128 devices in a mesh: col: 64 (over z, y, x_hi, core), seq: 2 (over x_lo).
Axes of the slice: x: 4 (x_hi: 2, x_lo: 2; x = x_hi * 2 + x_lo), y: 4, z: 4, core: 2. Of those that a mesh axis runs over, the one named last changes fastest.
Arguments:
- history_items: int32 [64, 1024], P(None, 'seq'), may hold values from 0 to 65535
- lengths: int32 [64], replicated, may hold values from 64 to 1024, as said below
- item_table: float32 [512, 65536], P('col'), may hold values from -4 to 4
- input_weight: bfloat16 [512, 2048], replicated, may hold values from -0.25 to 0.25
- output_weight: bfloat16 [512, 512], replicated, may hold values from -0.25 to 0.25
- output_cotangent: bfloat16 [64, 1024, 512], P('col', 'seq'), may hold values from -6 to 6
Outputs:
- layer_output: bfloat16 [64, 1024, 512], P('col', 'seq')
- table_gradient: float32 [512, 65536], P('col', 'seq')
The draws below stay inside these ranges and needn't reach their ends.
Inputs may be any that keep to these rules, and one draw needn't show every extreme that they name: `lengths`: in every draw one history has exactly 1024 items.
All inputs are finite; a program needn't handle non-finite values.
Results may differ from the reference program's by a relative error of at most 0.0077.
Values may be sent and summed in bfloat16 or wider, within the bound.
No kernel may reach another device: no remote copies, remote signals or barrier semaphores. Data moves between devices by JAX's collectives and lax.ppermute only.
A program may use at most 128 MiB of HBM per device.

```python
import math
import jax
import jax.numpy as jnp
import numpy as np
from jax import lax

D = 512
H = 8
DH = 64
LEN = 1024
TABLE_ROWS = 65536
USERS = 64


def draw_lengths(key, part):
    draw_key, pick_key = jax.random.split(key)
    drawn = jax.random.randint(draw_key, (USERS,), LEN // 16, LEN + 1, dtype=jnp.int32)
    longest = jax.random.randint(pick_key, (), 0, USERS, dtype=jnp.int32)
    return jnp.where(jnp.arange(USERS, dtype=jnp.int32) == longest, LEN, drawn).astype(jnp.int32)


def place_ends(values, stream_key, smallest, top_value):
    longest = values.shape.index(max(values.shape))
    spots = []
    for shift in (0, 1):
        where = [jax.random.randint(jax.random.fold_in(stream_key, axis), (), 0, length) for axis, length in enumerate(values.shape)]
        where[longest] = (where[longest] + shift) % values.shape[longest]
        spots.append(tuple(where))
    return values.at[spots[0]].set(smallest).at[spots[1]].set(top_value)


def shard_levels(stream_key, shape, cuts, least, high):
    level = 1.0
    for axis_at, blocks in cuts:
        heights = jax.random.uniform(jax.random.fold_in(jax.random.fold_in(stream_key, 6), axis_at), (blocks,), jnp.float32, least / len(cuts), high / len(cuts))
        level = level * jnp.repeat(jnp.exp(heights), shape[axis_at] // blocks).reshape((-1,) + (1,) * (len(shape) - 1 - axis_at))
    return level


def cumulative_ranks(number_of, slope):
    loads = [(1 << 20) // math.isqrt(standing ** slope) + 1 for standing in range(1, number_of + 1)]
    spread = 1 + sum(loads) // (1 << 30)
    return np.cumsum(np.array([max(1, weight // spread) for weight in loads]))


def skewed_ids(stream_key, shape, amount, skew):
    table = cumulative_ranks(amount, skew)
    pick = jax.random.randint(jax.random.fold_in(stream_key, 1), shape, 0, int(table[amount - 1]))
    standing = jnp.searchsorted(jnp.asarray(table, jnp.int32), pick, side="right")
    return jax.random.permutation(jax.random.fold_in(stream_key, 2), amount)[standing].astype(jnp.int32)


def centred(rng, shape, width, reach, cuts=(), held_as=jnp.bfloat16):
    result = jax.random.normal(rng, shape, jnp.float32) * width
    if len(cuts) > 0:
        result = shard_levels(rng, shape, cuts, -0.22, 0.18) * result
    return jnp.clip(result, min=-reach, max=reach).astype(held_as)


def setup_inputs(seed: int = 0) -> dict:
    seeds = jax.random.split(jax.random.key(seed), 7)
    return {
        "history_items": place_ends(skewed_ids(seeds[0], (USERS, LEN), TABLE_ROWS, 1), jax.random.fold_in(seeds[0], 3), 0, TABLE_ROWS - 1).astype(jnp.int32),
        "lengths": draw_lengths(jax.random.fold_in(seeds[6], 71), 0),
        "item_table": centred(seeds[2], (D, TABLE_ROWS), 0.5, 4.0, ((0, 64),), jnp.float32),
        "input_weight": centred(seeds[3], (D, 4 * H * DH), D ** -0.5, 0.25),
        "output_weight": centred(seeds[4], (H * DH, D), (H * DH) ** -0.5, 0.25),
        "output_cotangent": centred(seeds[5], (USERS, LEN, D), 1.0, 6.0, ((0, 64), (1, 2))),
    }


norm_epsilon = 1e-05

def layer_norm(inputs):
    average = lax.optimization_barrier(jnp.mean(inputs, axis=-1, keepdims=True))
    centered = inputs - average
    variance = lax.optimization_barrier(jnp.mean(centered * centered, axis=-1, keepdims=True))
    return centered * lax.rsqrt(variance + norm_epsilon)

def silu_slope(inputs):
    sigmoid_part = jax.nn.sigmoid(inputs)
    return sigmoid_part * (1.0 + inputs * (1.0 - sigmoid_part))

def one_user(item_table, input_weight, output_weight, item_row, length, grad_row):
    hidden = H * DH
    score_scale = DH ** (-0.5)
    length_scale = 1.0 / LEN
    looked = jnp.take(item_table, item_row, axis=1).T
    embedded = lax.optimization_barrier(looked.astype(jnp.bfloat16))
    features = embedded.astype(jnp.float32)
    normed = layer_norm(features).astype(jnp.bfloat16)
    preact = jnp.dot(normed, input_weight, preferred_element_type=jnp.float32)
    activated = jax.nn.silu(preact)
    update_part = activated[:, :hidden].astype(jnp.bfloat16)
    value_part = activated[:, hidden:2 * hidden].astype(jnp.bfloat16)
    query_part = activated[:, 2 * hidden:3 * hidden].astype(jnp.bfloat16)
    key_part = activated[:, 3 * hidden:].astype(jnp.bfloat16)
    query_heads = query_part.astype(jnp.float32).reshape(LEN, H, DH)
    key_heads = key_part.astype(jnp.float32).reshape(LEN, H, DH)
    value_heads = value_part.astype(jnp.float32).reshape(LEN, H, DH)
    positions = jnp.arange(LEN, dtype=jnp.int32)
    allowed = (positions[None, :] <= positions[:, None]) & (positions < length)[None, :]
    valid = positions < length
    scores = jnp.einsum('qhd,khd->hqk', query_heads, key_heads) * score_scale
    point_weights = jnp.where(allowed[None], jax.nn.silu(scores) * length_scale, 0.0).astype(jnp.bfloat16)
    attended = jnp.einsum('hqk,khd->qhd', point_weights.astype(jnp.float32), value_heads).reshape(LEN, hidden)
    normed_att = layer_norm(attended)
    gated = (normed_att * update_part.astype(jnp.float32)).astype(jnp.bfloat16)
    mixed = jnp.dot(gated, output_weight, preferred_element_type=jnp.float32) + features
    layer_output = jnp.where(valid[:, None], mixed, 0.0).astype(jnp.bfloat16)
    cotangent = jnp.where(valid[:, None], grad_row, jnp.zeros_like(grad_row))
    gated_grad = jnp.dot(cotangent, output_weight.T, preferred_element_type=jnp.float32)
    normed_grad = gated_grad * update_part.astype(jnp.float32)
    update_grad = gated_grad * normed_att
    attended_back = jax.vjp(layer_norm, attended)[1]
    attended_grad = attended_back(normed_grad)[0].astype(jnp.bfloat16)
    attended_heads = attended_grad.astype(jnp.float32).reshape(LEN, H, DH)
    weight_grad = jnp.einsum('qhd,khd->hqk', attended_heads, value_heads)
    score_grad = jnp.where(allowed[None], weight_grad * silu_slope(scores) * length_scale, 0.0).astype(jnp.bfloat16).astype(jnp.float32)
    query_grad = jnp.einsum('hqk,khd->qhd', score_grad, key_heads) * score_scale
    key_grad = jnp.einsum('hqk,qhd->khd', score_grad, query_heads) * score_scale
    value_grad = jnp.einsum('hqk,qhd->khd', point_weights.astype(jnp.float32), attended_heads)
    activation_grad = jnp.concatenate([update_grad, value_grad.reshape(LEN, hidden), query_grad.reshape(LEN, hidden), key_grad.reshape(LEN, hidden)], axis=-1)
    preact_grad = (activation_grad * silu_slope(preact)).astype(jnp.bfloat16)
    entry_grad = jnp.dot(preact_grad, input_weight.T, preferred_element_type=jnp.float32)
    features_back = jax.vjp(layer_norm, features)[1]
    input_grad = cotangent.astype(jnp.float32) + features_back(entry_grad)[0]
    return (layer_output, input_grad)

def reference(history_items, lengths, item_table, input_weight, output_weight, output_cotangent):

    def per_user(inputs):
        item_row, length, grad_row = inputs
        return one_user(item_table, input_weight, output_weight, item_row, length, grad_row)
    layer_output, input_grad = lax.map(per_user, (history_items, lengths, output_cotangent))
    table_gradient = jnp.zeros((D, TABLE_ROWS), jnp.float32).at[:, history_items.reshape(-1)].add(input_grad.reshape(-1, D).T)
    return (layer_output, table_gradient)
```

```python
import jax
import jax.numpy as jnp
from jax import lax
from jax.experimental import pallas as pl
from jax.experimental.pallas import tpu as pltpu
from jax.sharding import PartitionSpec as P

H = 8
DH = 64
LEN = 1024
D = 512
HID = H * DH
USERS = 64
FEAT = 8
HALF = 512
BLK = 128
NBLK = HALF // BLK
ROWS = 65536
PAIRS = H // 2
norm_epsilon = 1e-05
bf16 = jnp.bfloat16
f32 = jnp.float32

G_LO = 32
G_HI = ROWS // G_LO
G_STEP = 8
S_ROWS = ROWS // 2
S_LO = 32
S_HI = S_ROWS // S_LO
S_STEP = 16


def block_list(meta_ref, list_ref):
    seq = meta_ref[0]

    def step(u, count):
        parity = (seq + u) & 1
        blocks = (meta_ref[2 + u] + (BLK - 1)) // BLK
        for i in range(NBLK):
            list_ref[count + i] = u * NBLK + i
        return count + (blocks + 1 - parity) // 2

    return lax.fori_loop(0, USERS, step, 0)


def item_row(items_ref, seq, block):
    u = block // NBLK
    i = block % NBLK
    parity = (seq + u) & 1
    half = i // 2
    row = half * (USERS * NBLK) + u * NBLK + 2 * (i % 2) + parity
    return items_ref[pl.ds(row, 1), :]


def stage_items(seq, own_ref, other_ref, items_ref):
    n = USERS * NBLK
    items_ref[pl.ds(pl.multiple_of(seq * n, n), n), :] = own_ref[...]
    items_ref[pl.ds(pl.multiple_of((1 - seq) * n, n), n), :] = other_ref[...]


def onehot(index, rows):
    n = index.shape[1]
    iota = lax.broadcasted_iota(jnp.int16, (rows, n), 0)
    wide = jnp.broadcast_to(index.astype(jnp.int16), (rows, n))
    return jnp.where(iota == wide, jnp.ones((), bf16), jnp.zeros((), bf16))


def gather_kernel(meta_ref, own_ref, other_ref, table_ref, out_ref, t_ref, items_ref, list_ref):
    seq = meta_ref[0]
    stage_items(seq, own_ref, other_ref, items_ref)
    for lo in range(G_LO):
        t_ref[lo * FEAT : (lo + 1) * FEAT, :] = table_ref[:, lo * G_HI : (lo + 1) * G_HI].astype(bf16)
    out_ref[...] = jnp.zeros_like(out_ref)
    count = block_list(meta_ref, list_ref)

    def step(g, carry):
        ids = []
        for j in range(G_STEP):
            b = jnp.minimum(g * G_STEP + j, count - 1)
            ids.append(list_ref[jnp.maximum(b, 0)])
        index = jnp.concatenate([item_row(items_ref, seq, b) for b in ids], axis=1)
        lo = lax.shift_right_logical(index, 11)
        hi = index & (G_HI - 1)
        acc = jnp.dot(t_ref[...], onehot(hi, G_HI), preferred_element_type=f32)
        n = G_STEP * BLK
        acc = acc.reshape(G_LO, FEAT, n)
        mask = lax.broadcasted_iota(jnp.int32, (G_LO, FEAT, n), 0) == lo.reshape(1, 1, n)
        picked = jnp.sum(jnp.where(mask, acc, 0.0), axis=0).astype(bf16)
        for j in range(G_STEP):
            u = ids[j] // NBLK
            col = pl.multiple_of((ids[j] % NBLK) * BLK, BLK)
            part = picked[:, j * BLK : (j + 1) * BLK]
            out_ref[u, 0, :, pl.ds(col, BLK)] = part
            out_ref[u, 1, :, pl.ds(col, BLK)] = part
        return carry

    lax.fori_loop(0, (count + G_STEP - 1) // G_STEP, step, 0)


def scatter_kernel(meta_ref, half_ref, own_ref, other_ref, grad_ref, out_ref, items_ref, acc_ref, list_ref):
    seq = meta_ref[0]
    base = half_ref[0] * S_ROWS
    stage_items(seq, own_ref, other_ref, items_ref)
    acc_ref[...] = jnp.zeros_like(acc_ref)
    count = block_list(meta_ref, list_ref)

    def step(g, carry):
        rows, grads = [], []
        for j in range(S_STEP):
            at = g * S_STEP + j
            b = list_ref[jnp.maximum(jnp.minimum(at, count - 1), 0)]
            row = item_row(items_ref, seq, b) - base
            rows.append(jnp.where(at < count, row, -1))
            u = b // NBLK
            col = pl.multiple_of((b % NBLK) * BLK, BLK)
            grads.append(
                grad_ref[u, 0, :, pl.ds(col, BLK)].astype(f32)
                + grad_ref[u, 1, :, pl.ds(col, BLK)].astype(f32)
            )
        index = jnp.concatenate(rows, axis=1)
        grad = jnp.concatenate(grads, axis=1)
        n = S_STEP * BLK
        lo = lax.shift_right_arithmetic(index, 10)
        hi = index & (S_HI - 1)
        mask = lax.broadcasted_iota(jnp.int32, (S_LO, FEAT, n), 0) == lo.reshape(1, 1, n)
        spread = jnp.where(mask, jnp.broadcast_to(grad[None], (S_LO, FEAT, n)), 0.0)
        spread = spread.reshape(S_LO * FEAT, n).astype(bf16)
        acc_ref[...] += lax.dot_general(
            spread, onehot(hi, S_HI), (((1,), (1,)), ((), ())), preferred_element_type=f32
        )
        return carry

    lax.fori_loop(0, (count + S_STEP - 1) // S_STEP, step, 0)
    for lo in range(S_LO):
        out_ref[:, lo * S_HI : (lo + 1) * S_HI] = acc_ref[lo * FEAT : (lo + 1) * FEAT, :].astype(
            out_ref.dtype
        )


def dot_nt(a, b):
    return lax.dot_general(a, b, (((1,), (1,)), ((), ())), preferred_element_type=f32)


def dot_tn(a, b):
    return lax.dot_general(a, b, (((0,), (0,)), ((), ())), preferred_element_type=f32)


def dot_nn(a, b):
    return jnp.dot(a, b, preferred_element_type=f32)


def norm(z):
    m = jnp.mean(z, axis=-1, keepdims=True)
    c = z - m
    w = jnp.mean(c * c, axis=-1, keepdims=True)
    r = lax.rsqrt(w + norm_epsilon)
    return c * r, r


def norm_back(y, r, dy):
    a = jnp.mean(dy, axis=-1, keepdims=True)
    b = jnp.mean(dy * y, axis=-1, keepdims=True)
    return r * (dy - a - y * b)


def sigmoid(x):
    return 0.5 * jnp.tanh(0.5 * x) + 0.5


def layer_kernel(
    meta_ref, e_ref, w_ref, wo_ref, cot_ref, out_ref, g_ref,
    x_ref, y_ref, r_ref, yl_ref, rl_ref, slope_ref, slopel_ref, u_ref, q_ref, k_ref, v_ref,
    p_ref, d_ref, pl_ref, dl_ref, att_ref, do_ref, pg_ref, pgl_ref,
):
    seq = meta_ref[0]
    col = meta_ref[1]
    length = meta_ref[2 + col]
    base = seq * HALF
    upper = seq == 1
    active = length > base
    lanes = lax.broadcasted_iota(jnp.int32, (1, 2 * DH), 1)
    head_mask = [(lanes < DH).astype(f32).astype(bf16), (lanes >= DH).astype(f32).astype(bf16)]

    def place(half, b):
        i = 2 * half + b // 2
        return (b + col) & 1, pl.multiple_of(i * BLK, BLK)

    def features(half):
        parts = []
        for b in range(NBLK):
            src, at = place(half, b)
            part = e_ref[:, src, :, pl.ds(at, BLK)].astype(f32).reshape(D, BLK)
            parts.append(part.T)
        return jnp.concatenate(parts, axis=0)

    def put_grad(half, grad):
        flat = grad.T.reshape(D // FEAT, FEAT, HALF).astype(bf16)
        for b in range(NBLK):
            dst, at = place(half, b)
            g_ref[:, dst, :, pl.ds(at, BLK)] = flat[:, :, b * BLK : (b + 1) * BLK]

    def activate(pre):
        s = sigmoid(pre)
        act = pre * s
        return act, s + act * (1.0 - s)

    g_ref[...] = jnp.zeros_like(g_ref)

    @pl.when(jnp.logical_not(active))
    def _():
        out_ref[...] = jnp.zeros_like(out_ref)

    @pl.when(active)
    def _():
        x = features(seq)
        x_ref[...] = x
        y, r = norm(x)
        y_ref[...] = y
        r_ref[...] = r
        yb = y.astype(bf16)
        for blk in range(4):
            act, slope = activate(dot_nn(yb, w_ref[:, blk * HID : (blk + 1) * HID]))
            slope_ref[:, blk * HID : (blk + 1) * HID] = slope
            if blk == 2:
                act = act.astype(bf16).astype(f32) * (DH**-0.5)
            act = act.astype(bf16)
            if blk == 0:
                u_ref[...] = act
            else:
                for hp in range(PAIRS):
                    part = act[:, hp * 2 * DH : (hp + 1) * 2 * DH]
                    if blk == 1:
                        v_ref[1, hp] = part
                    elif blk == 2:
                        q_ref[hp] = part
                    else:
                        k_ref[1, hp] = part

        @pl.when(upper)
        def _():
            y, r = norm(features(0))
            yl_ref[...] = y
            rl_ref[...] = r
            yb = y.astype(bf16)
            for n, blk in enumerate((1, 3)):
                act, slope = activate(dot_nn(yb, w_ref[:, blk * HID : (blk + 1) * HID]))
                slopel_ref[:, n * HID : (n + 1) * HID] = slope
                act = act.astype(bf16)
                for hp in range(PAIRS):
                    part = act[:, hp * 2 * DH : (hp + 1) * 2 * DH]
                    if n == 0:
                        v_ref[0, hp] = part
                    else:
                        k_ref[0, hp] = part

        def weights(scores, limit):
            s = sigmoid(scores)
            act = scores * s
            slope = s + act * (1.0 - s)
            if limit is not None:
                ok = lax.broadcasted_iota(jnp.int32, scores.shape, 1) <= limit
                act = jnp.where(ok, act, 0.0)
                slope = jnp.where(ok, slope, 0.0)
            return (act * (1.0 / LEN)).astype(bf16), slope * (1.0 / LEN)

        QB = HALF // 2
        row = lax.broadcasted_iota(jnp.int32, (QB, 1), 0)

        @pl.loop(0, PAIRS)
        def _(hp):
            q, k, v = q_ref[hp], k_ref[1, hp], v_ref[1, hp]
            att = [None, None]
            for h in range(2):
                vm = v * head_mask[h]
                for qi in range(2):
                    qb = q[qi * QB : (qi + 1) * QB] * head_mask[h]
                    for ki in range(qi + 1):
                        scores = dot_nt(qb, k[ki * QB : (ki + 1) * QB])
                        limit = None
                        if ki == qi:
                            limit = jnp.minimum(row, length - 1 - base - ki * QB)
                        p, d = weights(scores, limit)
                        at = 2 * qi + ki
                        p_ref[2 * hp + h, at] = p
                        d_ref[2 * hp + h, at] = d
                        add = dot_nn(p, vm[ki * QB : (ki + 1) * QB])
                        att[qi] = add if att[qi] is None else att[qi] + add
            att_ref[hp] = jnp.concatenate(att, axis=0)

            @pl.when(upper)
            def _():
                kl, vl = k_ref[0, hp], v_ref[0, hp]
                for h in range(2):
                    scores = dot_nt(q * head_mask[h], kl)
                    p, d = weights(scores, None)
                    pl_ref[2 * hp + h] = p
                    dl_ref[2 * hp + h] = d
                    att_ref[hp] += dot_nn(p, vl * head_mask[h])

        att = jnp.concatenate([att_ref[hp] for hp in range(PAIRS)], axis=1)
        na, ra = norm(att)
        u = u_ref[...].astype(f32)
        valid = (base + lax.broadcasted_iota(jnp.int32, (HALF, 1), 0)) < length
        mixed = dot_nn((na * u).astype(bf16), wo_ref[...]) + x_ref[...]
        out_ref[...] = jnp.where(valid, mixed, 0.0).astype(bf16)
        cot = jnp.where(valid, cot_ref[...].astype(f32), 0.0)
        gg = dot_nt(cot.astype(bf16), wo_ref[...])
        pg_ref[:, :HID] = (gg * na * slope_ref[:, :HID]).astype(bf16)
        da = norm_back(na, ra, gg * u).astype(bf16)
        for hp in range(PAIRS):
            do_ref[hp] = da[:, hp * 2 * DH : (hp + 1) * 2 * DH]

        @pl.loop(0, PAIRS)
        def _(hp):
            q, k, v, do = q_ref[hp], k_ref[1, hp], v_ref[1, hp], do_ref[hp]
            dq = [None, None]
            dk = [None, None]
            dv = [None, None]

            def plus(a, b):
                return b if a is None else a + b

            for h in range(2):
                km = k * head_mask[h]
                qm = q * head_mask[h]
                dm = do * head_mask[h]
                for qi in range(2):
                    qs = slice(qi * QB, (qi + 1) * QB)
                    for ki in range(qi + 1):
                        ks = slice(ki * QB, (ki + 1) * QB)
                        at = 2 * qi + ki
                        ds = (dot_nt(dm[qs], v[ks]) * d_ref[2 * hp + h, at]).astype(bf16)
                        dq[qi] = plus(dq[qi], dot_nn(ds, km[ks]))
                        dk[ki] = plus(dk[ki], dot_tn(ds, qm[qs]))
                        dv[ki] = plus(dv[ki], dot_tn(p_ref[2 * hp + h, at], dm[qs]))
            at = pl.multiple_of(hp * 2 * DH, 2 * DH)
            vs = pl.ds(HID + at, 2 * DH)
            qs_ = pl.ds(2 * HID + at, 2 * DH)
            ks_ = pl.ds(3 * HID + at, 2 * DH)
            pg_ref[:, vs] = (jnp.concatenate(dv, axis=0) * slope_ref[:, vs]).astype(bf16)
            pg_ref[:, ks_] = (jnp.concatenate(dk, axis=0) * slope_ref[:, ks_]).astype(bf16)
            att_ref[hp] = jnp.concatenate(dq, axis=0)

            @pl.when(upper)
            def _():
                kl, vl = k_ref[0, hp], v_ref[0, hp]
                dkl, dvl = None, None
                for h in range(2):
                    dm = do * head_mask[h]
                    ds = (dot_nt(dm, vl) * dl_ref[2 * hp + h]).astype(bf16)
                    att_ref[hp] += dot_nn(ds, kl * head_mask[h])
                    dkl = plus(dkl, dot_tn(ds, q * head_mask[h]))
                    dvl = plus(dvl, dot_tn(pl_ref[2 * hp + h], dm))
                vl_ = pl.ds(at, 2 * DH)
                kl_ = pl.ds(HID + at, 2 * DH)
                pgl_ref[:, vl_] = (dvl * slopel_ref[:, vl_]).astype(bf16)
                pgl_ref[:, kl_] = (dkl * slopel_ref[:, kl_]).astype(bf16)

            pg_ref[:, qs_] = (att_ref[hp] * (DH**-0.5) * slope_ref[:, qs_]).astype(bf16)

        eg = dot_nt(pg_ref[...], w_ref[...])
        cot = jnp.where(valid, cot_ref[...].astype(f32), 0.0)
        put_grad(seq, cot + norm_back(y_ref[...], r_ref[...], eg))

        @pl.when(upper)
        def _():
            eg = dot_nt(pgl_ref[:, :HID], w_ref[:, HID : 2 * HID])
            eg = eg + dot_nt(pgl_ref[:, HID:], w_ref[:, 3 * HID :])
            put_grad(0, norm_back(yl_ref[...], rl_ref[...], eg))


def vmem():
    return pl.BlockSpec(memory_space=pltpu.VMEM)


def smem():
    return pl.BlockSpec(memory_space=pltpu.SMEM)


def params():
    return pltpu.CompilerParams(vmem_limit_bytes=60 * 1024 * 1024)


def gather(meta, own, other, table):
    return pl.pallas_call(
        gather_kernel,
        in_specs=[smem(), vmem(), vmem(), vmem()],
        out_specs=vmem(),
        out_shape=jax.ShapeDtypeStruct((USERS, 2, FEAT, HALF), bf16),
        scratch_shapes=[
            pltpu.VMEM((G_LO * FEAT, G_HI), bf16),
            pltpu.VMEM((2 * USERS * NBLK, BLK), jnp.int32),
            pltpu.SMEM((USERS * NBLK + NBLK,), jnp.int32),
        ],
        compiler_params=params(),
        name="gather",
    )(meta, own, other, table)


def scatter(meta, half, own, other, grad, dtype):
    return pl.pallas_call(
        scatter_kernel,
        in_specs=[smem(), smem(), vmem(), vmem(), vmem()],
        out_specs=vmem(),
        out_shape=jax.ShapeDtypeStruct((FEAT, S_ROWS), dtype),
        scratch_shapes=[
            pltpu.VMEM((2 * USERS * NBLK, BLK), jnp.int32),
            pltpu.VMEM((S_LO * FEAT, S_HI), f32),
            pltpu.SMEM((USERS * NBLK + NBLK,), jnp.int32),
        ],
        compiler_params=params(),
        name="scatter",
    )(meta, half, own, other, grad)


def layer(meta, e, w, wo, cot):
    return pl.pallas_call(
        layer_kernel,
        in_specs=[smem(), vmem(), vmem(), vmem(), vmem()],
        out_specs=(vmem(), vmem()),
        out_shape=(
            jax.ShapeDtypeStruct((HALF, D), bf16),
            jax.ShapeDtypeStruct((USERS, 2, FEAT, HALF), bf16),
        ),
        scratch_shapes=[
            pltpu.VMEM((HALF, D), f32),
            pltpu.VMEM((HALF, D), f32),
            pltpu.VMEM((HALF, 1), f32),
            pltpu.VMEM((HALF, D), f32),
            pltpu.VMEM((HALF, 1), f32),
            pltpu.VMEM((HALF, 4 * HID), f32),
            pltpu.VMEM((HALF, 2 * HID), f32),
            pltpu.VMEM((HALF, HID), bf16),
            pltpu.VMEM((PAIRS, HALF, 2 * DH), bf16),
            pltpu.VMEM((2, PAIRS, HALF, 2 * DH), bf16),
            pltpu.VMEM((2, PAIRS, HALF, 2 * DH), bf16),
            pltpu.VMEM((H, 4, HALF // 2, HALF // 2), bf16),
            pltpu.VMEM((H, 4, HALF // 2, HALF // 2), f32),
            pltpu.VMEM((H, HALF, HALF), bf16),
            pltpu.VMEM((H, HALF, HALF), f32),
            pltpu.VMEM((PAIRS, HALF, 2 * DH), f32),
            pltpu.VMEM((PAIRS, HALF, 2 * DH), bf16),
            pltpu.VMEM((HALF, 4 * HID), bf16),
            pltpu.VMEM((HALF, 2 * HID), bf16),
        ],
        compiler_params=params(),
        name="layer",
    )(meta, e, w, wo, cot)


def per_device(history_items, lengths, item_table, input_weight, output_weight, output_cotangent):
    col = lax.axis_index("col").astype(jnp.int32)
    seq = lax.axis_index("seq").astype(jnp.int32)
    meta = jnp.concatenate([jnp.stack([seq, col]), lengths])
    own = history_items.reshape(USERS * NBLK, BLK)
    other = lax.ppermute(own, "seq", [(0, 1), (1, 0)])
    looked = gather(meta, own, other, item_table)
    both = ("col", "seq")
    flat = looked.reshape(2 * USERS, FEAT, HALF)
    arrived = lax.all_to_all(flat, both, split_axis=0, concat_axis=0, tiled=True)
    arrived = arrived.reshape(USERS, 2, FEAT, HALF)
    out, grad = layer(meta, arrived, input_weight, output_weight, output_cotangent[0])
    grad = grad.reshape(2 * USERS, FEAT, HALF)
    back = lax.all_to_all(grad, both, split_axis=0, concat_axis=0, tiled=True)
    back = back.reshape(USERS, 2, FEAT, HALF)
    theirs = scatter(meta, (1 - seq).reshape(1), own, other, back, bf16)
    received = lax.ppermute(theirs, "seq", [(0, 1), (1, 0)])
    mine = scatter(meta, seq.reshape(1), own, other, back, f32)
    return (out[None], mine + received.astype(f32))


def solution(mesh):
    in_specs = (P(None, "seq"), P(), P("col", None), P(), P(), P("col", "seq", None))
    out_specs = (P("col", "seq", None), P("col", "seq"))
    return jax.shard_map(
        per_device, mesh=mesh, in_specs=in_specs, out_specs=out_specs, check_vma=False
    )
```

```python
import jax
import jax.numpy as jnp
from jax import lax
from jax.experimental import pallas as pl
from jax.experimental.pallas import tpu as pltpu
from jax.sharding import PartitionSpec as P

H = 8
DH = 64
LEN = 1024
D = 512
HID = H * DH
USERS = 64
FEAT = 8
HALF = 512
BLK = 128
NBLK = HALF // BLK
ROWS = 65536
PAIRS = H // 2
norm_epsilon = 1e-05
bf16 = jnp.bfloat16
f32 = jnp.float32

G_LO = 16
G_HI = ROWS // G_LO
G_STEP = 8
S_ROWS = ROWS // 2
S_LO = 32
S_HI = S_ROWS // S_LO
S_STEP = 16


def block_list(seq, lengths_ref, list_ref):
    def step(u, count):
        parity = (seq + u) & 1
        blocks = (lengths_ref[u] + (BLK - 1)) // BLK
        for i in range(NBLK):
            list_ref[count + i] = u * NBLK + i
        return count + (blocks + 1 - parity) // 2

    return lax.fori_loop(0, USERS, step, 0)


def item_row(items_ref, seq, block):
    u = block // NBLK
    i = block % NBLK
    parity = (seq + u) & 1
    return items_ref[i // 2, 2 * (i % 2) + parity, pl.ds(u, 1), :]


def stage_items(seq, own_ref, other_ref, items_ref):
    for b in range(NBLK):
        items_ref[seq, b] = own_ref[:, b * BLK : (b + 1) * BLK]
        items_ref[1 - seq, b] = other_ref[:, b * BLK : (b + 1) * BLK]


def onehot(index, rows):
    n = index.shape[1]
    iota = lax.broadcasted_iota(jnp.int16, (rows, n), 0)
    wide = jnp.broadcast_to(index.astype(jnp.int16), (rows, n))
    return jnp.where(iota == wide, jnp.ones((), bf16), jnp.zeros((), bf16))


def rows_kernel(table_ref, rows_ref):
    step = 512
    for c in range(G_HI // step):
        parts = [
            table_ref[:, lo * G_HI + c * step : lo * G_HI + (c + 1) * step] for lo in range(G_LO)
        ]
        rows_ref[c * step : (c + 1) * step, :] = jnp.concatenate(parts, axis=0).T


def gather_kernel(
    seq_ref, lengths_ref, own_ref, other_ref, rows_ref, out_ref,
    items_ref, stage_ref, got_ref, list_ref, index_ref, sems,
):
    seq = seq_ref[0]
    stage_items(seq, own_ref, other_ref, items_ref)
    out_ref[...] = jnp.zeros_like(out_ref)
    count = block_list(seq, lengths_ref, list_ref)
    pairs = (count + 2 * G_STEP - 1) // (2 * G_STEP)

    def ids_of(g):
        last = count - 1
        return [list_ref[jnp.minimum(g * G_STEP + j, last)] for j in range(G_STEP)]

    def copy(slot):
        return pltpu.make_async_copy(stage_ref.at[slot], index_ref.at[slot], sems.at[slot])

    def fetch(g, slot):
        rows = jnp.concatenate([item_row(items_ref, seq, b) for b in ids_of(g)], axis=0)
        stage_ref[slot] = rows & (G_HI - 1)
        copy(slot).start()

    def move(slot):
        for j in range(G_STEP):
            for t in range(BLK):
                r = index_ref[slot, j, t]
                got_ref[slot, pl.ds(j * BLK + t, 1), :] = rows_ref[pl.ds(r, 1), :]

    def finish(g, slot):
        ids = ids_of(g)
        for j in range(G_STEP):
            u = ids[j] // NBLK
            col = pl.multiple_of((ids[j] % NBLK) * BLK, BLK)
            lo = lax.shift_right_logical(item_row(items_ref, seq, ids[j]), 12)
            part = got_ref[slot, j * BLK : (j + 1) * BLK, :].T.reshape(G_LO, FEAT, BLK)
            mask = lax.broadcasted_iota(jnp.int32, (G_LO, FEAT, BLK), 0) == lo.reshape(1, 1, BLK)
            part = jnp.sum(jnp.where(mask, part, 0.0), axis=0).astype(bf16)
            out_ref[u, 0, :, pl.ds(col, BLK)] = part
            out_ref[u, 1, :, pl.ds(col, BLK)] = part

    got_ref[1] = jnp.zeros_like(got_ref[1])
    for slot in range(2):
        fetch(slot, slot)

    def step(p, carry):
        for slot in range(2):
            g = 2 * p + slot
            copy(slot).wait()
            move(slot)
            finish(jnp.maximum(g - 1, 0), 1 - slot)
            fetch(g + 2, slot)
        return carry

    lax.fori_loop(0, pairs, step, 0)
    finish(2 * pairs - 1, 1)
    for slot in range(2):
        copy(slot).wait()


def scatter_kernel(
    seq_ref, lengths_ref, half_ref, own_ref, other_ref, grad_ref, out_ref, items_ref, acc_ref, list_ref
):
    seq = seq_ref[0]
    base = half_ref[0] * S_ROWS
    stage_items(seq, own_ref, other_ref, items_ref)
    acc_ref[...] = jnp.zeros_like(acc_ref)
    count = block_list(seq, lengths_ref, list_ref)

    def step(g, carry):
        rows, grads = [], []
        for j in range(S_STEP):
            at = g * S_STEP + j
            b = list_ref[jnp.maximum(jnp.minimum(at, count - 1), 0)]
            row = item_row(items_ref, seq, b) - base
            rows.append(jnp.where(at < count, row, -1))
            u = b // NBLK
            col = pl.multiple_of((b % NBLK) * BLK, BLK)
            grads.append(
                grad_ref[u, 0, :, pl.ds(col, BLK)].astype(f32)
                + grad_ref[u, 1, :, pl.ds(col, BLK)].astype(f32)
            )
        index = jnp.concatenate(rows, axis=1)
        grad = jnp.concatenate(grads, axis=1)
        n = S_STEP * BLK
        lo = lax.shift_right_arithmetic(index, 10)
        hi = index & (S_HI - 1)
        mask = lax.broadcasted_iota(jnp.int32, (S_LO, FEAT, n), 0) == lo.reshape(1, 1, n)
        spread = jnp.where(mask, jnp.broadcast_to(grad[None], (S_LO, FEAT, n)), 0.0)
        spread = spread.reshape(S_LO * FEAT, n).astype(bf16)
        acc_ref[...] += lax.dot_general(
            spread, onehot(hi, S_HI), (((1,), (1,)), ((), ())), preferred_element_type=f32
        )
        return carry

    lax.fori_loop(0, (count + S_STEP - 1) // S_STEP, step, 0)
    for lo in range(S_LO):
        out_ref[:, lo * S_HI : (lo + 1) * S_HI] = acc_ref[lo * FEAT : (lo + 1) * FEAT, :].astype(
            out_ref.dtype
        )


def dot_nt(a, b):
    return lax.dot_general(a, b, (((1,), (1,)), ((), ())), preferred_element_type=f32)


def dot_tn(a, b):
    return lax.dot_general(a, b, (((0,), (0,)), ((), ())), preferred_element_type=f32)


def dot_nn(a, b):
    return jnp.dot(a, b, preferred_element_type=f32)


def norm(z):
    m = jnp.mean(z, axis=-1, keepdims=True)
    c = z - m
    w = jnp.mean(c * c, axis=-1, keepdims=True)
    r = lax.rsqrt(w + norm_epsilon)
    return c * r, r


def norm_back(y, r, dy):
    a = jnp.mean(dy, axis=-1, keepdims=True)
    b = jnp.mean(dy * y, axis=-1, keepdims=True)
    return r * (dy - a - y * b)


def sigmoid(x):
    return 0.5 * jnp.tanh(0.5 * x) + 0.5


def layer_kernel(
    seq_ref, col_ref, lengths_ref, e_ref, w_ref, wo_ref, cot_ref, out_ref, g_ref,
    x_ref, y_ref, r_ref, yl_ref, rl_ref, slope_ref, slopel_ref, u_ref, q_ref, k_ref, v_ref,
    p_ref, d_ref, pl_ref, dl_ref, att_ref, do_ref, pg_ref, pgl_ref,
):
    seq = seq_ref[0]
    col = col_ref[0]
    length = lengths_ref[col]
    base = seq * HALF
    upper = seq == 1
    active = length > base
    lanes = lax.broadcasted_iota(jnp.int32, (1, 2 * DH), 1)
    head_mask = [(lanes < DH).astype(f32).astype(bf16), (lanes >= DH).astype(f32).astype(bf16)]

    def place(half, b):
        i = 2 * half + b // 2
        return (b + col) & 1, pl.multiple_of(i * BLK, BLK)

    def features(half):
        parts = []
        for b in range(NBLK):
            src, at = place(half, b)
            part = e_ref[:, src, :, pl.ds(at, BLK)].astype(f32).reshape(D, BLK)
            parts.append(part.T)
        return jnp.concatenate(parts, axis=0)

    def put_grad(half, grad):
        flat = grad.T.reshape(D // FEAT, FEAT, HALF).astype(bf16)
        for b in range(NBLK):
            dst, at = place(half, b)
            g_ref[:, dst, :, pl.ds(at, BLK)] = flat[:, :, b * BLK : (b + 1) * BLK]

    def activate(pre):
        s = sigmoid(pre)
        act = pre * s
        return act, s + act * (1.0 - s)

    g_ref[...] = jnp.zeros_like(g_ref)

    @pl.when(jnp.logical_not(active))
    def _():
        out_ref[...] = jnp.zeros_like(out_ref)

    @pl.when(active)
    def _():
        x = features(seq)
        x_ref[...] = x
        y, r = norm(x)
        y_ref[...] = y
        r_ref[...] = r
        yb = y.astype(bf16)
        for blk in range(4):
            act, slope = activate(dot_nn(yb, w_ref[:, blk * HID : (blk + 1) * HID]))
            slope_ref[:, blk * HID : (blk + 1) * HID] = slope
            if blk == 2:
                act = act.astype(bf16).astype(f32) * (DH**-0.5)
            act = act.astype(bf16)
            if blk == 0:
                u_ref[...] = act
            else:
                for hp in range(PAIRS):
                    part = act[:, hp * 2 * DH : (hp + 1) * 2 * DH]
                    if blk == 1:
                        v_ref[1, hp] = part
                    elif blk == 2:
                        q_ref[hp] = part
                    else:
                        k_ref[1, hp] = part

        @pl.when(upper)
        def _():
            y, r = norm(features(0))
            yl_ref[...] = y
            rl_ref[...] = r
            yb = y.astype(bf16)
            for n, blk in enumerate((1, 3)):
                act, slope = activate(dot_nn(yb, w_ref[:, blk * HID : (blk + 1) * HID]))
                slopel_ref[:, n * HID : (n + 1) * HID] = slope
                act = act.astype(bf16)
                for hp in range(PAIRS):
                    part = act[:, hp * 2 * DH : (hp + 1) * 2 * DH]
                    if n == 0:
                        v_ref[0, hp] = part
                    else:
                        k_ref[0, hp] = part

        def weights(scores, limit):
            s = sigmoid(scores)
            act = scores * s
            slope = s + act * (1.0 - s)
            if limit is not None:
                ok = lax.broadcasted_iota(jnp.int32, scores.shape, 1) <= limit
                act = jnp.where(ok, act, 0.0)
                slope = jnp.where(ok, slope, 0.0)
            return (act * (1.0 / LEN)).astype(bf16), slope * (1.0 / LEN)

        QB = HALF // 2
        row = lax.broadcasted_iota(jnp.int32, (QB, 1), 0)

        @pl.loop(0, PAIRS)
        def _(hp):
            q, k, v = q_ref[hp], k_ref[1, hp], v_ref[1, hp]
            att = [None, None]
            for h in range(2):
                vm = v * head_mask[h]
                for qi in range(2):
                    qb = q[qi * QB : (qi + 1) * QB] * head_mask[h]
                    for ki in range(qi + 1):
                        scores = dot_nt(qb, k[ki * QB : (ki + 1) * QB])
                        limit = None
                        if ki == qi:
                            limit = jnp.minimum(row, length - 1 - base - ki * QB)
                        p, d = weights(scores, limit)
                        at = 2 * qi + ki
                        p_ref[2 * hp + h, at] = p
                        d_ref[2 * hp + h, at] = d
                        add = dot_nn(p, vm[ki * QB : (ki + 1) * QB])
                        att[qi] = add if att[qi] is None else att[qi] + add
            att_ref[hp] = jnp.concatenate(att, axis=0)

            @pl.when(upper)
            def _():
                kl, vl = k_ref[0, hp], v_ref[0, hp]
                for h in range(2):
                    scores = dot_nt(q * head_mask[h], kl)
                    p, d = weights(scores, None)
                    pl_ref[2 * hp + h] = p
                    dl_ref[2 * hp + h] = d
                    att_ref[hp] += dot_nn(p, vl * head_mask[h])

        att = jnp.concatenate([att_ref[hp] for hp in range(PAIRS)], axis=1)
        na, ra = norm(att)
        u = u_ref[...].astype(f32)
        valid = (base + lax.broadcasted_iota(jnp.int32, (HALF, 1), 0)) < length
        mixed = dot_nn((na * u).astype(bf16), wo_ref[...]) + x_ref[...]
        out_ref[...] = jnp.where(valid, mixed, 0.0).astype(bf16)
        cot = jnp.where(valid, cot_ref[...].astype(f32), 0.0)
        gg = dot_nt(cot.astype(bf16), wo_ref[...])
        pg_ref[:, :HID] = (gg * na * slope_ref[:, :HID]).astype(bf16)
        da = norm_back(na, ra, gg * u).astype(bf16)
        for hp in range(PAIRS):
            do_ref[hp] = da[:, hp * 2 * DH : (hp + 1) * 2 * DH]

        @pl.loop(0, PAIRS)
        def _(hp):
            q, k, v, do = q_ref[hp], k_ref[1, hp], v_ref[1, hp], do_ref[hp]
            dq = [None, None]
            dk = [None, None]
            dv = [None, None]

            def plus(a, b):
                return b if a is None else a + b

            for h in range(2):
                km = k * head_mask[h]
                qm = q * head_mask[h]
                dm = do * head_mask[h]
                for qi in range(2):
                    qs = slice(qi * QB, (qi + 1) * QB)
                    for ki in range(qi + 1):
                        ks = slice(ki * QB, (ki + 1) * QB)
                        at = 2 * qi + ki
                        ds = (dot_nt(dm[qs], v[ks]) * d_ref[2 * hp + h, at]).astype(bf16)
                        dq[qi] = plus(dq[qi], dot_nn(ds, km[ks]))
                        dk[ki] = plus(dk[ki], dot_tn(ds, qm[qs]))
                        dv[ki] = plus(dv[ki], dot_tn(p_ref[2 * hp + h, at], dm[qs]))
            at = pl.multiple_of(hp * 2 * DH, 2 * DH)
            vs = pl.ds(HID + at, 2 * DH)
            qs_ = pl.ds(2 * HID + at, 2 * DH)
            ks_ = pl.ds(3 * HID + at, 2 * DH)
            pg_ref[:, vs] = (jnp.concatenate(dv, axis=0) * slope_ref[:, vs]).astype(bf16)
            pg_ref[:, ks_] = (jnp.concatenate(dk, axis=0) * slope_ref[:, ks_]).astype(bf16)
            att_ref[hp] = jnp.concatenate(dq, axis=0)

            @pl.when(upper)
            def _():
                kl, vl = k_ref[0, hp], v_ref[0, hp]
                dkl, dvl = None, None
                for h in range(2):
                    dm = do * head_mask[h]
                    ds = (dot_nt(dm, vl) * dl_ref[2 * hp + h]).astype(bf16)
                    att_ref[hp] += dot_nn(ds, kl * head_mask[h])
                    dkl = plus(dkl, dot_tn(ds, q * head_mask[h]))
                    dvl = plus(dvl, dot_tn(pl_ref[2 * hp + h], dm))
                vl_ = pl.ds(at, 2 * DH)
                kl_ = pl.ds(HID + at, 2 * DH)
                pgl_ref[:, vl_] = (dvl * slopel_ref[:, vl_]).astype(bf16)
                pgl_ref[:, kl_] = (dkl * slopel_ref[:, kl_]).astype(bf16)

            pg_ref[:, qs_] = (att_ref[hp] * (DH**-0.5) * slope_ref[:, qs_]).astype(bf16)

        eg = dot_nt(pg_ref[...], w_ref[...])
        cot = jnp.where(valid, cot_ref[...].astype(f32), 0.0)
        put_grad(seq, cot + norm_back(y_ref[...], r_ref[...], eg))

        @pl.when(upper)
        def _():
            eg = dot_nt(pgl_ref[:, :HID], w_ref[:, HID : 2 * HID])
            eg = eg + dot_nt(pgl_ref[:, HID:], w_ref[:, 3 * HID :])
            put_grad(0, norm_back(yl_ref[...], rl_ref[...], eg))


def vmem():
    return pl.BlockSpec(memory_space=pltpu.VMEM)


def smem():
    return pl.BlockSpec(memory_space=pltpu.SMEM)


def params():
    return pltpu.CompilerParams(vmem_limit_bytes=60 * 1024 * 1024)


def table_rows(table):
    return pl.pallas_call(
        rows_kernel,
        in_specs=[vmem()],
        out_specs=vmem(),
        out_shape=jax.ShapeDtypeStruct((G_HI, BLK), f32),
        compiler_params=params(),
        name="table_rows",
    )(table)


def gather(seq, lengths, own, other, rows):
    return pl.pallas_call(
        gather_kernel,
        in_specs=[smem(), smem(), vmem(), vmem(), vmem()],
        out_specs=vmem(),
        out_shape=jax.ShapeDtypeStruct((USERS, 2, FEAT, HALF), bf16),
        scratch_shapes=[
            pltpu.VMEM((2, NBLK, USERS, BLK), jnp.int32),
            pltpu.VMEM((2, G_STEP, BLK), jnp.int32),
            pltpu.VMEM((2, G_STEP * BLK, BLK), f32),
            pltpu.SMEM((USERS * NBLK + NBLK,), jnp.int32),
            pltpu.SMEM((2, G_STEP, BLK), jnp.int32),
            pltpu.SemaphoreType.DMA((2,)),
        ],
        compiler_params=params(),
        name="gather",
    )(seq, lengths, own, other, rows)


def scatter(seq, lengths, half, own, other, grad, dtype):
    return pl.pallas_call(
        scatter_kernel,
        in_specs=[smem(), smem(), smem(), vmem(), vmem(), vmem()],
        out_specs=vmem(),
        out_shape=jax.ShapeDtypeStruct((FEAT, S_ROWS), dtype),
        scratch_shapes=[
            pltpu.VMEM((2, NBLK, USERS, BLK), jnp.int32),
            pltpu.VMEM((S_LO * FEAT, S_HI), f32),
            pltpu.SMEM((USERS * NBLK + NBLK,), jnp.int32),
        ],
        compiler_params=params(),
        name="scatter",
    )(seq, lengths, half, own, other, grad)


def layer(seq, col, lengths, e, w, wo, cot):
    return pl.pallas_call(
        layer_kernel,
        in_specs=[smem(), smem(), smem(), vmem(), vmem(), vmem(), vmem()],
        out_specs=(vmem(), vmem()),
        out_shape=(
            jax.ShapeDtypeStruct((HALF, D), bf16),
            jax.ShapeDtypeStruct((USERS, 2, FEAT, HALF), bf16),
        ),
        scratch_shapes=[
            pltpu.VMEM((HALF, D), f32),
            pltpu.VMEM((HALF, D), f32),
            pltpu.VMEM((HALF, 1), f32),
            pltpu.VMEM((HALF, D), f32),
            pltpu.VMEM((HALF, 1), f32),
            pltpu.VMEM((HALF, 4 * HID), f32),
            pltpu.VMEM((HALF, 2 * HID), f32),
            pltpu.VMEM((HALF, HID), bf16),
            pltpu.VMEM((PAIRS, HALF, 2 * DH), bf16),
            pltpu.VMEM((2, PAIRS, HALF, 2 * DH), bf16),
            pltpu.VMEM((2, PAIRS, HALF, 2 * DH), bf16),
            pltpu.VMEM((H, 4, HALF // 2, HALF // 2), bf16),
            pltpu.VMEM((H, 4, HALF // 2, HALF // 2), f32),
            pltpu.VMEM((H, HALF, HALF), bf16),
            pltpu.VMEM((H, HALF, HALF), f32),
            pltpu.VMEM((PAIRS, HALF, 2 * DH), f32),
            pltpu.VMEM((PAIRS, HALF, 2 * DH), bf16),
            pltpu.VMEM((HALF, 4 * HID), bf16),
            pltpu.VMEM((HALF, 2 * HID), bf16),
        ],
        compiler_params=params(),
        name="layer",
    )(seq, col, lengths, e, w, wo, cot)


def per_device(history_items, lengths, item_table, input_weight, output_weight, output_cotangent):
    col = lax.axis_index("col").astype(jnp.int32).reshape(1)
    seq = lax.axis_index("seq").astype(jnp.int32).reshape(1)
    swap = [(0, 1), (1, 0)]
    both = ("col", "seq")
    own = history_items
    other = lax.ppermute(own, "seq", swap)
    rows = table_rows(item_table)
    looked = gather(seq, lengths, own, other, rows)
    flat = looked.reshape(2 * USERS, FEAT, HALF)
    arrived = lax.all_to_all(flat, both, split_axis=0, concat_axis=0, tiled=True)
    arrived = arrived.reshape(USERS, 2, FEAT, HALF)
    out, grad = layer(
        seq, col, lengths, arrived, input_weight, output_weight, output_cotangent[0]
    )
    grad = grad.reshape(2 * USERS, FEAT, HALF)
    back = lax.all_to_all(grad, both, split_axis=0, concat_axis=0, tiled=True)
    back = back.reshape(USERS, 2, FEAT, HALF)
    theirs = scatter(seq, lengths, 1 - seq, own, other, back, bf16)
    received = lax.ppermute(theirs, "seq", swap)
    mine = scatter(seq, lengths, seq, own, other, back, f32)
    return (out[None], mine + received.astype(f32))


def solution(mesh):
    in_specs = (P(None, "seq"), P(), P("col", None), P(), P(), P("col", "seq", None))
    out_specs = (P("col", "seq", None), P("col", "seq"))
    return jax.shard_map(
        per_device, mesh=mesh, in_specs=in_specs, out_specs=out_specs, check_vma=False
    )
```

```python
import jax
import jax.numpy as jnp
from jax import lax
from jax.experimental import pallas as pl
from jax.experimental.pallas import tpu as pltpu
from jax.sharding import PartitionSpec as P

H = 8
DH = 64
LEN = 1024
D = 512
HID = H * DH
USERS = 64
FEAT = 8
HALF = 512
BLK = 128
NBLK = HALF // BLK
ROWS = 65536
PAIRS = H // 2
norm_epsilon = 1e-05
bf16 = jnp.bfloat16
f32 = jnp.float32

G_LO = 16
G_HI = ROWS // G_LO
G_STEP = 8
S_ROWS = ROWS // 2
S_LO = 32
S_HI = S_ROWS // S_LO
S_STEP = 16


def block_list(seq, lengths_ref, list_ref):
    def step(u, count):
        parity = (seq + u) & 1
        blocks = (lengths_ref[u] + (BLK - 1)) // BLK
        for i in range(NBLK):
            list_ref[count + i] = u * NBLK + i
        return count + (blocks + 1 - parity) // 2

    return lax.fori_loop(0, USERS, step, 0)


def item_row(items_ref, seq, block):
    u = block // NBLK
    i = block % NBLK
    parity = (seq + u) & 1
    return items_ref[i // 2, 2 * (i % 2) + parity, pl.ds(u, 1), :]


def stage_items(seq, own_ref, other_ref, items_ref):
    for b in range(NBLK):
        items_ref[seq, b] = own_ref[:, b * BLK : (b + 1) * BLK]
        items_ref[1 - seq, b] = other_ref[:, b * BLK : (b + 1) * BLK]


def onehot(index, rows):
    n = index.shape[1]
    iota = lax.broadcasted_iota(jnp.int16, (rows, n), 0)
    wide = jnp.broadcast_to(index.astype(jnp.int16), (rows, n))
    return jnp.where(iota == wide, jnp.ones((), bf16), jnp.zeros((), bf16))


def rows_kernel(table_ref, rows_ref):
    step = 512
    for c in range(G_HI // step):
        parts = [
            table_ref[:, lo * G_HI + c * step : lo * G_HI + (c + 1) * step] for lo in range(G_LO)
        ]
        rows_ref[c * step : (c + 1) * step, :] = jnp.concatenate(parts, axis=0).T


def gather_kernel(
    seq_ref, lengths_ref, own_ref, other_ref, rows_ref, out_ref,
    items_ref, stage_ref, got_ref, list_ref, index_ref, sems,
):
    seq = seq_ref[0]
    stage_items(seq, own_ref, other_ref, items_ref)
    out_ref[...] = jnp.zeros_like(out_ref)
    count = block_list(seq, lengths_ref, list_ref)
    pairs = (count + 2 * G_STEP - 1) // (2 * G_STEP)

    def ids_of(g):
        last = count - 1
        return [list_ref[jnp.minimum(g * G_STEP + j, last)] for j in range(G_STEP)]

    def copy(slot):
        return pltpu.make_async_copy(stage_ref.at[slot], index_ref.at[slot], sems.at[slot])

    def fetch(g, slot):
        rows = jnp.concatenate([item_row(items_ref, seq, b) for b in ids_of(g)], axis=0)
        stage_ref[slot] = rows & (G_HI - 1)
        copy(slot).start()

    def move(slot):
        for j in range(G_STEP):
            for t in range(BLK):
                r = index_ref[slot, j, t]
                got_ref[slot, pl.ds(j * BLK + t, 1), :] = rows_ref[pl.ds(r, 1), :]

    def finish(g, slot):
        ids = ids_of(g)
        for j in range(G_STEP):
            u = ids[j] // NBLK
            col = pl.multiple_of((ids[j] % NBLK) * BLK, BLK)
            lo = lax.shift_right_logical(item_row(items_ref, seq, ids[j]), 12)
            part = got_ref[slot, j * BLK : (j + 1) * BLK, :].T.reshape(G_LO, FEAT, BLK)
            mask = lax.broadcasted_iota(jnp.int32, (G_LO, FEAT, BLK), 0) == lo.reshape(1, 1, BLK)
            part = jnp.sum(jnp.where(mask, part, 0.0), axis=0).astype(bf16)
            out_ref[u, 0, :, pl.ds(col, BLK)] = part
            out_ref[u, 1, :, pl.ds(col, BLK)] = part

    got_ref[1] = jnp.zeros_like(got_ref[1])
    for slot in range(2):
        fetch(slot, slot)

    def step(p, carry):
        for slot in range(2):
            g = 2 * p + slot
            copy(slot).wait()
            move(slot)
            finish(jnp.maximum(g - 1, 0), 1 - slot)
            fetch(g + 2, slot)
        return carry

    lax.fori_loop(0, pairs, step, 0)
    finish(2 * pairs - 1, 1)
    for slot in range(2):
        copy(slot).wait()


def scatter_kernel(
    seq_ref, lengths_ref, half_ref, own_ref, other_ref, grad_ref, out_ref, items_ref, acc_ref, list_ref
):
    seq = seq_ref[0]
    base = half_ref[0] * S_ROWS
    stage_items(seq, own_ref, other_ref, items_ref)
    acc_ref[...] = jnp.zeros_like(acc_ref)
    count = block_list(seq, lengths_ref, list_ref)

    def step(g, carry):
        rows, grads = [], []
        for j in range(S_STEP):
            at = g * S_STEP + j
            b = list_ref[jnp.maximum(jnp.minimum(at, count - 1), 0)]
            row = item_row(items_ref, seq, b) - base
            rows.append(jnp.where(at < count, row, -1))
            u = b // NBLK
            col = pl.multiple_of((b % NBLK) * BLK, BLK)
            grads.append(
                grad_ref[u, 0, :, pl.ds(col, BLK)].astype(f32)
                + grad_ref[u, 1, :, pl.ds(col, BLK)].astype(f32)
            )
        index = jnp.concatenate(rows, axis=1)
        grad = jnp.concatenate(grads, axis=1)
        n = S_STEP * BLK
        lo = lax.shift_right_arithmetic(index, 10)
        hi = index & (S_HI - 1)
        mask = lax.broadcasted_iota(jnp.int32, (S_LO, FEAT, n), 0) == lo.reshape(1, 1, n)
        spread = jnp.where(mask, jnp.broadcast_to(grad[None], (S_LO, FEAT, n)), 0.0)
        spread = spread.reshape(S_LO * FEAT, n).astype(bf16)
        acc_ref[...] += lax.dot_general(
            spread, onehot(hi, S_HI), (((1,), (1,)), ((), ())), preferred_element_type=f32
        )
        return carry

    lax.fori_loop(0, (count + S_STEP - 1) // S_STEP, step, 0)
    for lo in range(S_LO):
        out_ref[:, lo * S_HI : (lo + 1) * S_HI] = acc_ref[lo * FEAT : (lo + 1) * FEAT, :].astype(
            out_ref.dtype
        )


def dot_nt(a, b):
    return lax.dot_general(a, b, (((1,), (1,)), ((), ())), preferred_element_type=f32)


def dot_nn(a, b):
    return jnp.dot(a, b, preferred_element_type=f32)


def norm(z):
    m = jnp.mean(z, axis=-1, keepdims=True)
    c = z - m
    w = jnp.mean(c * c, axis=-1, keepdims=True)
    r = lax.rsqrt(w + norm_epsilon)
    return c * r, r


def norm_back(y, r, dy):
    a = jnp.mean(dy, axis=-1, keepdims=True)
    b = jnp.mean(dy * y, axis=-1, keepdims=True)
    return r * (dy - a - y * b)


def gate(h):
    t = jnp.tanh(h)
    a = 1.0 + t
    act = h * a
    return act, a + act * (1.0 - t)


def layer_kernel(
    seq_ref, col_ref, lengths_ref, e_ref, w_ref, wo_ref, cot_ref, out_ref, g_ref,
    x_ref, y_ref, r_ref, yl_ref, rl_ref, slope_ref, slopel_ref, u_ref, q_ref, qt_ref, k_ref, kt_ref, v_ref, vt_ref,
    p_ref, d_ref, pl_ref, dl_ref, att_ref, do_ref, dot_ref, dk_ref, dv_ref, dkl_ref, dvl_ref,
    pg_ref, pgl_ref,
):
    seq = seq_ref[0]
    col = col_ref[0]
    length = lengths_ref[col]
    base = seq * HALF
    upper = seq == 1
    active = length > base
    lanes = lax.broadcasted_iota(jnp.int32, (1, 2 * DH), 1)
    head_mask = [(lanes < DH).astype(f32).astype(bf16), (lanes >= DH).astype(f32).astype(bf16)]
    QB = HALF // 2
    parts = [slice(0, QB), slice(QB, HALF)]

    def place(half, b):
        i = 2 * half + b // 2
        return (b + col) & 1, pl.multiple_of(i * BLK, BLK)

    def features(half):
        parts = []
        for b in range(NBLK):
            src, at = place(half, b)
            part = e_ref[:, src, :, pl.ds(at, BLK)].astype(f32).reshape(D, BLK)
            parts.append(part.T)
        return jnp.concatenate(parts, axis=0)

    def put_grad(half, grad):
        flat = grad.T.reshape(D // FEAT, FEAT, HALF).astype(bf16)
        for b in range(NBLK):
            dst, at = place(half, b)
            g_ref[:, dst, :, pl.ds(at, BLK)] = flat[:, :, b * BLK : (b + 1) * BLK]

    def pairs_of(act):
        return [act[:, hp * 2 * DH : (hp + 1) * 2 * DH] for hp in range(PAIRS)]

    def project(half, blocks, yb, slopes):
        for n, blk in enumerate(blocks):
            act, slope = gate(dot_nn(yb, w_ref[:, blk * HID : (blk + 1) * HID]))
            slopes[:, n * HID : (n + 1) * HID] = slope
            act = act.astype(bf16)
            if blk == 0:
                u_ref[...] = act
            elif blk == 2:
                act = act.astype(f32) * (0.5 * DH**-0.5)
                qt_ref[...] = act.T.astype(bf16)
                for hp, part in enumerate(pairs_of(act.astype(bf16))):
                    q_ref[hp] = part
            else:
                target, turned = (v_ref, vt_ref) if blk == 1 else (k_ref, kt_ref)
                turned[half] = act.T
                for hp, part in enumerate(pairs_of(act)):
                    target[half, hp] = part

    def plus(a, b):
        return b if a is None else a + b

    def forward(hp, lower):
        q, k = q_ref[hp], k_ref[1, hp]
        if lower:
            kl = k_ref[0, hp]
        row = lax.broadcasted_iota(jnp.int32, (QB, 1), 0)
        for h in range(2):
            head = 2 * hp + h
            hs = pl.ds(pl.multiple_of(head * DH, DH), DH)
            vt = vt_ref[1, hs, :]
            qm = q * head_mask[h]
            att = [None, None]
            for qi in range(2):
                for ki in range(qi + 1):
                    act, slope = gate(dot_nt(qm[parts[qi]], k[parts[ki]]))
                    if ki == qi:
                        limit = jnp.minimum(row, length - 1 - base - ki * QB)
                        ok = lax.broadcasted_iota(jnp.int32, act.shape, 1) <= limit
                        act = jnp.where(ok, act, 0.0)
                        slope = jnp.where(ok, slope, 0.0)
                    at = 2 * qi + ki
                    p = act.astype(bf16)
                    p_ref[head, at] = p
                    d_ref[head, at] = slope
                    att[qi] = plus(att[qi], dot_nt(vt[:, parts[ki]], p))
                if lower:
                    act, slope = gate(dot_nt(qm[parts[qi]], kl))
                    p = act.astype(bf16)
                    pl_ref[head, parts[qi]] = p
                    dl_ref[head, parts[qi]] = slope
                    att[qi] = att[qi] + dot_nt(vt_ref[0, hs, :], p)
            att_ref[hs, :] = jnp.concatenate(att, axis=1)

    def backward(hp, lower):
        v, do = v_ref[1, hp], do_ref[hp]
        if lower:
            vl = v_ref[0, hp]
        for h in range(2):
            head = 2 * hp + h
            hs = pl.ds(pl.multiple_of(head * DH, DH), DH)
            qt = qt_ref[hs, :]
            dot = dot_ref[hs, :]
            kt = kt_ref[1, hs, :]
            dm = do * head_mask[h]
            dq = [None, None]
            dk = [None, None]
            dv = [None, None]
            if lower:
                dkl, dvl = None, None
            for qi in range(2):
                qs = parts[qi]
                for ki in range(qi + 1):
                    at = 2 * qi + ki
                    ds = (dot_nt(dm[qs], v[parts[ki]]) * d_ref[head, at]).astype(bf16)
                    dq[qi] = plus(dq[qi], dot_nt(kt[:, parts[ki]], ds))
                    dk[ki] = plus(dk[ki], dot_nn(qt[:, qs], ds))
                    dv[ki] = plus(dv[ki], dot_nn(dot[:, qs], p_ref[head, at]))
                if lower:
                    ds = (dot_nt(dm[qs], vl) * dl_ref[head, qs]).astype(bf16)
                    dq[qi] = plus(dq[qi], dot_nt(kt_ref[0, hs, :], ds))
                    dkl = plus(dkl, dot_nn(qt[:, qs], ds))
                    dvl = plus(dvl, dot_nn(dot[:, qs], pl_ref[head, qs]))
            att_ref[hs, :] = jnp.concatenate(dq, axis=1)
            dk_ref[hs, :] = jnp.concatenate(dk, axis=1)
            dv_ref[hs, :] = jnp.concatenate(dv, axis=1)
            if lower:
                dkl_ref[hs, :] = dkl
                dvl_ref[hs, :] = dvl

    def over_pairs(body):
        @pl.when(upper)
        def _():
            @pl.loop(0, PAIRS)
            def _(hp):
                body(hp, True)

        @pl.when(jnp.logical_not(upper))
        def _():
            @pl.loop(0, PAIRS)
            def _(hp):
                body(hp, False)

    g_ref[...] = jnp.zeros_like(g_ref)

    @pl.when(jnp.logical_not(active))
    def _():
        out_ref[...] = jnp.zeros_like(out_ref)

    @pl.when(active)
    def _():
        x = features(seq)
        x_ref[...] = x
        y, r = norm(x)
        y_ref[...] = y
        r_ref[...] = 0.5 * r
        project(1, (0, 1, 2, 3), (0.5 * y).astype(bf16), slope_ref)

        @pl.when(upper)
        def _():
            y, r = norm(features(0))
            yl_ref[...] = y
            rl_ref[...] = 0.5 * r
            project(0, (1, 3), (0.5 * y).astype(bf16), slopel_ref)

        over_pairs(forward)

        na, ra = norm(att_ref[...].T * (1.0 / LEN))
        u = u_ref[...].astype(f32)
        valid = (base + lax.broadcasted_iota(jnp.int32, (HALF, 1), 0)) < length
        mixed = dot_nn((na * u).astype(bf16), wo_ref[...]) + x_ref[...]
        out_ref[...] = jnp.where(valid, mixed, 0.0).astype(bf16)
        cot = jnp.where(valid, cot_ref[...].astype(f32), 0.0)
        gg = dot_nt(cot.astype(bf16), wo_ref[...])
        pg_ref[:, :HID] = (gg * na * slope_ref[:, :HID]).astype(bf16)
        da = norm_back(na, ra * (1.0 / LEN), gg * u)
        dot_ref[...] = da.T.astype(bf16)
        for hp, part in enumerate(pairs_of(da.astype(bf16))):
            do_ref[hp] = part

        over_pairs(backward)

        dq = att_ref[...].T * (0.5 * DH**-0.5)
        pg_ref[:, HID : 2 * HID] = (dv_ref[...].T * slope_ref[:, HID : 2 * HID]).astype(bf16)
        pg_ref[:, 2 * HID : 3 * HID] = (dq * slope_ref[:, 2 * HID : 3 * HID]).astype(bf16)
        pg_ref[:, 3 * HID :] = (dk_ref[...].T * slope_ref[:, 3 * HID :]).astype(bf16)
        eg = dot_nt(pg_ref[...], w_ref[...])
        cot = jnp.where(valid, cot_ref[...].astype(f32), 0.0)
        put_grad(seq, cot + norm_back(y_ref[...], r_ref[...], eg))

        @pl.when(upper)
        def _():
            pgl_ref[:, :HID] = (dvl_ref[...].T * slopel_ref[:, :HID]).astype(bf16)
            pgl_ref[:, HID:] = (dkl_ref[...].T * slopel_ref[:, HID:]).astype(bf16)
            eg = dot_nt(pgl_ref[:, :HID], w_ref[:, HID : 2 * HID])
            eg = eg + dot_nt(pgl_ref[:, HID:], w_ref[:, 3 * HID :])
            put_grad(0, norm_back(yl_ref[...], rl_ref[...], eg))


def vmem():
    return pl.BlockSpec(memory_space=pltpu.VMEM)


def smem():
    return pl.BlockSpec(memory_space=pltpu.SMEM)


def params():
    return pltpu.CompilerParams(vmem_limit_bytes=60 * 1024 * 1024)


def table_rows(table):
    return pl.pallas_call(
        rows_kernel,
        in_specs=[vmem()],
        out_specs=vmem(),
        out_shape=jax.ShapeDtypeStruct((G_HI, BLK), f32),
        compiler_params=params(),
        name="table_rows",
    )(table)


def gather(seq, lengths, own, other, rows):
    return pl.pallas_call(
        gather_kernel,
        in_specs=[smem(), smem(), vmem(), vmem(), vmem()],
        out_specs=vmem(),
        out_shape=jax.ShapeDtypeStruct((USERS, 2, FEAT, HALF), bf16),
        scratch_shapes=[
            pltpu.VMEM((2, NBLK, USERS, BLK), jnp.int32),
            pltpu.VMEM((2, G_STEP, BLK), jnp.int32),
            pltpu.VMEM((2, G_STEP * BLK, BLK), f32),
            pltpu.SMEM((USERS * NBLK + NBLK,), jnp.int32),
            pltpu.SMEM((2, G_STEP, BLK), jnp.int32),
            pltpu.SemaphoreType.DMA((2,)),
        ],
        compiler_params=params(),
        name="gather",
    )(seq, lengths, own, other, rows)


def scatter(seq, lengths, half, own, other, grad, dtype):
    return pl.pallas_call(
        scatter_kernel,
        in_specs=[smem(), smem(), smem(), vmem(), vmem(), vmem()],
        out_specs=vmem(),
        out_shape=jax.ShapeDtypeStruct((FEAT, S_ROWS), dtype),
        scratch_shapes=[
            pltpu.VMEM((2, NBLK, USERS, BLK), jnp.int32),
            pltpu.VMEM((S_LO * FEAT, S_HI), f32),
            pltpu.SMEM((USERS * NBLK + NBLK,), jnp.int32),
        ],
        compiler_params=params(),
        name="scatter",
    )(seq, lengths, half, own, other, grad)


def layer(seq, col, lengths, e, w, wo, cot):
    return pl.pallas_call(
        layer_kernel,
        in_specs=[smem(), smem(), smem(), vmem(), vmem(), vmem(), vmem()],
        out_specs=(vmem(), vmem()),
        out_shape=(
            jax.ShapeDtypeStruct((HALF, D), bf16),
            jax.ShapeDtypeStruct((USERS, 2, FEAT, HALF), bf16),
        ),
        scratch_shapes=[
            pltpu.VMEM((HALF, D), f32),
            pltpu.VMEM((HALF, D), f32),
            pltpu.VMEM((HALF, 1), f32),
            pltpu.VMEM((HALF, D), f32),
            pltpu.VMEM((HALF, 1), f32),
            pltpu.VMEM((HALF, 4 * HID), f32),
            pltpu.VMEM((HALF, 2 * HID), f32),
            pltpu.VMEM((HALF, HID), bf16),
            pltpu.VMEM((PAIRS, HALF, 2 * DH), bf16),
            pltpu.VMEM((HID, HALF), bf16),
            pltpu.VMEM((2, PAIRS, HALF, 2 * DH), bf16),
            pltpu.VMEM((2, HID, HALF), bf16),
            pltpu.VMEM((2, PAIRS, HALF, 2 * DH), bf16),
            pltpu.VMEM((2, HID, HALF), bf16),
            pltpu.VMEM((H, 4, HALF // 2, HALF // 2), bf16),
            pltpu.VMEM((H, 4, HALF // 2, HALF // 2), f32),
            pltpu.VMEM((H, HALF, HALF), bf16),
            pltpu.VMEM((H, HALF, HALF), f32),
            pltpu.VMEM((HID, HALF), f32),
            pltpu.VMEM((PAIRS, HALF, 2 * DH), bf16),
            pltpu.VMEM((HID, HALF), bf16),
            pltpu.VMEM((HID, HALF), f32),
            pltpu.VMEM((HID, HALF), f32),
            pltpu.VMEM((HID, HALF), f32),
            pltpu.VMEM((HID, HALF), f32),
            pltpu.VMEM((HALF, 4 * HID), bf16),
            pltpu.VMEM((HALF, 2 * HID), bf16),
        ],
        compiler_params=params(),
        name="layer",
    )(seq, col, lengths, e, w, wo, cot)


def per_device(history_items, lengths, item_table, input_weight, output_weight, output_cotangent):
    col = lax.axis_index("col").astype(jnp.int32).reshape(1)
    seq = lax.axis_index("seq").astype(jnp.int32).reshape(1)
    swap = [(0, 1), (1, 0)]
    both = ("col", "seq")
    own = history_items
    other = lax.ppermute(own, "seq", swap)
    rows = table_rows(item_table)
    looked = gather(seq, lengths, own, other, rows)
    flat = looked.reshape(2 * USERS, FEAT, HALF)
    arrived = lax.all_to_all(flat, both, split_axis=0, concat_axis=0, tiled=True)
    arrived = arrived.reshape(USERS, 2, FEAT, HALF)
    out, grad = layer(
        seq, col, lengths, arrived, input_weight, output_weight, output_cotangent[0]
    )
    grad = grad.reshape(2 * USERS, FEAT, HALF)
    back = lax.all_to_all(grad, both, split_axis=0, concat_axis=0, tiled=True)
    back = back.reshape(USERS, 2, FEAT, HALF)
    theirs = scatter(seq, lengths, 1 - seq, own, other, back, bf16)
    received = lax.ppermute(theirs, "seq", swap)
    mine = scatter(seq, lengths, seq, own, other, back, f32)
    return (out[None], mine + received.astype(f32))


def solution(mesh):
    in_specs = (P(None, "seq"), P(), P("col", None), P(), P(), P("col", "seq", None))
    out_specs = (P("col", "seq", None), P("col", "seq"))
    return jax.shard_map(
        per_device, mesh=mesh, in_specs=in_specs, out_specs=out_specs, check_vma=False
    )
```

```python
import jax
import jax.numpy as jnp
from jax import lax
from jax.experimental import pallas as pl
from jax.experimental.pallas import tpu as pltpu
from jax.sharding import PartitionSpec as P

H = 8
DH = 64
LEN = 1024
D = 512
HID = H * DH
USERS = 64
FEAT = 8
HALF = 512
BLK = 128
NBLK = HALF // BLK
ROWS = 65536
PAIRS = H // 2
norm_epsilon = 1e-05
bf16 = jnp.bfloat16
f32 = jnp.float32

G_LO = 16
G_HI = ROWS // G_LO
G_STEP = 8
S_ROWS = ROWS // 2
S_LO = 32
S_HI = S_ROWS // S_LO
S_STEP = 16


def block_list(seq, lengths_ref, list_ref):
    def step(u, count):
        parity = (seq + u) & 1
        blocks = (lengths_ref[u] + (BLK - 1)) >> 7
        for i in range(NBLK):
            list_ref[count + i] = u * NBLK + i
        return count + ((blocks + 1 - parity) >> 1)

    return lax.fori_loop(0, USERS, step, 0)


def item_row(items_ref, seq, block):
    u = block >> 2
    i = block & 3
    parity = (seq + u) & 1
    return items_ref[i >> 1, 2 * (i & 1) + parity, pl.ds(u, 1), :]


def stage_items(seq, own_ref, other_ref, items_ref):
    for b in range(NBLK):
        items_ref[seq, b] = own_ref[:, b * BLK : (b + 1) * BLK]
        items_ref[1 - seq, b] = other_ref[:, b * BLK : (b + 1) * BLK]


def onehot(index, rows):
    n = index.shape[1]
    iota = lax.broadcasted_iota(jnp.int16, (rows, n), 0)
    wide = jnp.broadcast_to(index.astype(jnp.int16), (rows, n))
    return jnp.where(iota == wide, jnp.ones((), bf16), jnp.zeros((), bf16))


def rows_kernel(table_ref, rows_ref):
    step = 512
    for c in range(G_HI // step):
        parts = [
            table_ref[:, lo * G_HI + c * step : lo * G_HI + (c + 1) * step] for lo in range(G_LO)
        ]
        rows_ref[c * step : (c + 1) * step, :] = jnp.concatenate(parts, axis=0).T


def gather_kernel(
    seq_ref, lengths_ref, own_ref, other_ref, rows_ref, out_ref,
    items_ref, stage_ref, got_ref, list_ref, index_ref, sems,
):
    seq = seq_ref[0]
    stage_items(seq, own_ref, other_ref, items_ref)
    out_ref[...] = jnp.zeros_like(out_ref)
    count = block_list(seq, lengths_ref, list_ref)
    pairs = (count + 2 * G_STEP - 1) // (2 * G_STEP)

    def ids_of(g):
        last = count - 1
        return [list_ref[jnp.minimum(g * G_STEP + j, last)] for j in range(G_STEP)]

    def copy(slot):
        return pltpu.make_async_copy(stage_ref.at[slot], index_ref.at[slot], sems.at[slot])

    def fetch(g, slot):
        rows = jnp.concatenate([item_row(items_ref, seq, b) for b in ids_of(g)], axis=0)
        stage_ref[slot] = rows & (G_HI - 1)
        copy(slot).start()

    def move(slot):
        for j in range(G_STEP):
            for t in range(BLK):
                r = index_ref[slot, j, t]
                got_ref[slot, pl.ds(j * BLK + t, 1), :] = rows_ref[pl.ds(r, 1), :]

    def finish(g, slot):
        ids = ids_of(g)
        for j in range(G_STEP):
            u = ids[j] >> 2
            col = pl.multiple_of((ids[j] & 3) * BLK, BLK)
            lo = lax.shift_right_logical(item_row(items_ref, seq, ids[j]), 12)
            part = got_ref[slot, j * BLK : (j + 1) * BLK, :].T.reshape(G_LO, FEAT, BLK)
            mask = lax.broadcasted_iota(jnp.int32, (G_LO, FEAT, BLK), 0) == lo.reshape(1, 1, BLK)
            part = jnp.sum(jnp.where(mask, part, 0.0), axis=0).astype(bf16)
            out_ref[u, 0, :, pl.ds(col, BLK)] = part
            out_ref[u, 1, :, pl.ds(col, BLK)] = part

    got_ref[1] = jnp.zeros_like(got_ref[1])
    for slot in range(2):
        fetch(slot, slot)

    def step(p, carry):
        for slot in range(2):
            g = 2 * p + slot
            copy(slot).wait()
            move(slot)
            finish(jnp.maximum(g - 1, 0), 1 - slot)
            fetch(g + 2, slot)
        return carry

    lax.fori_loop(0, pairs, step, 0)
    finish(2 * pairs - 1, 1)
    for slot in range(2):
        copy(slot).wait()


def scatter_kernel(
    seq_ref, lengths_ref, half_ref, own_ref, other_ref, grad_ref, out_ref, items_ref, acc_ref, list_ref
):
    seq = seq_ref[0]
    base = half_ref[0] * S_ROWS
    stage_items(seq, own_ref, other_ref, items_ref)
    acc_ref[...] = jnp.zeros_like(acc_ref)
    count = block_list(seq, lengths_ref, list_ref)

    def step(g, carry):
        rows, grads = [], []
        for j in range(S_STEP):
            at = g * S_STEP + j
            b = list_ref[jnp.maximum(jnp.minimum(at, count - 1), 0)]
            row = item_row(items_ref, seq, b) - base
            rows.append(jnp.where(at < count, row, -1))
            u = b >> 2
            col = pl.multiple_of((b & 3) * BLK, BLK)
            grads.append(
                grad_ref[u, 0, :, pl.ds(col, BLK)].astype(f32)
                + grad_ref[u, 1, :, pl.ds(col, BLK)].astype(f32)
            )
        index = jnp.concatenate(rows, axis=1)
        grad = jnp.concatenate(grads, axis=1)
        n = S_STEP * BLK
        lo = lax.shift_right_arithmetic(index, 10)
        hi = index & (S_HI - 1)
        mask = lax.broadcasted_iota(jnp.int32, (S_LO, FEAT, n), 0) == lo.reshape(1, 1, n)
        spread = jnp.where(mask, jnp.broadcast_to(grad[None], (S_LO, FEAT, n)), 0.0)
        spread = spread.reshape(S_LO * FEAT, n).astype(bf16)
        acc_ref[...] += lax.dot_general(
            spread, onehot(hi, S_HI), (((1,), (1,)), ((), ())), preferred_element_type=f32
        )
        return carry

    lax.fori_loop(0, (count + S_STEP - 1) // S_STEP, step, 0)
    for lo in range(S_LO):
        out_ref[:, lo * S_HI : (lo + 1) * S_HI] = acc_ref[lo * FEAT : (lo + 1) * FEAT, :].astype(
            out_ref.dtype
        )


def dot_nt(a, b):
    return lax.dot_general(a, b, (((1,), (1,)), ((), ())), preferred_element_type=f32)


def dot_nn(a, b):
    return jnp.dot(a, b, preferred_element_type=f32)


def norm(z):
    m = jnp.mean(z, axis=-1, keepdims=True)
    c = z - m
    w = jnp.mean(c * c, axis=-1, keepdims=True)
    r = lax.rsqrt(w + norm_epsilon)
    return c * r, r


def norm_back(y, r, dy):
    a = jnp.mean(dy, axis=-1, keepdims=True)
    b = jnp.mean(dy * y, axis=-1, keepdims=True)
    return r * (dy - a - y * b)


def gate(h):
    t = jnp.tanh(h)
    a = 1.0 + t
    act = h * a
    return act, a + act * (1.0 - t)


def layer_kernel(
    seq_ref, col_ref, lengths_ref, e_ref, w_hbm, wo_hbm, cot_hbm, out_ref, g_ref,
    w_ref, wo_ref, cot_ref, sems,
    x_ref, y_ref, r_ref, yl_ref, rl_ref, slope_ref, slopel_ref, u_ref, q_ref, qt_ref, k_ref, kt_ref, v_ref, vt_ref,
    p_ref, d_ref, pl_ref, dl_ref, att_ref, do_ref, dot_ref, dk_ref, dv_ref, dkl_ref, dvl_ref,
    pg_ref, pgl_ref,
):
    seq = seq_ref[0]
    col = col_ref[0]
    length = lengths_ref[col]
    base = seq * HALF
    upper = seq == 1
    active = length > base
    lanes = lax.broadcasted_iota(jnp.int32, (1, 2 * DH), 1)
    head_mask = [(lanes < DH).astype(f32).astype(bf16), (lanes >= DH).astype(f32).astype(bf16)]
    loads = [
        pltpu.make_async_copy(src, dst, sems.at[n])
        for n, (src, dst) in enumerate(((w_hbm, w_ref), (wo_hbm, wo_ref), (cot_hbm, cot_ref)))
    ]
    for load in loads:
        load.start()
    QB = HALF // 2
    parts = [slice(0, QB), slice(QB, HALF)]

    def place(half, b):
        i = 2 * half + b // 2
        return (b + col) & 1, pl.multiple_of(i * BLK, BLK)

    def features(half):
        parts = []
        for b in range(NBLK):
            src, at = place(half, b)
            part = e_ref[:, src, :, pl.ds(at, BLK)].astype(f32).reshape(D, BLK)
            parts.append(part.T)
        return jnp.concatenate(parts, axis=0)

    def put_grad(half, grad):
        flat = grad.T.reshape(D // FEAT, FEAT, HALF).astype(bf16)
        for b in range(NBLK):
            dst, at = place(half, b)
            g_ref[:, dst, :, pl.ds(at, BLK)] = flat[:, :, b * BLK : (b + 1) * BLK]

    def pairs_of(act):
        return [act[:, hp * 2 * DH : (hp + 1) * 2 * DH] for hp in range(PAIRS)]

    def project(half, blocks, yb, slopes):
        for n, blk in enumerate(blocks):
            act, slope = gate(dot_nn(yb, w_ref[:, blk * HID : (blk + 1) * HID]))
            slopes[:, n * HID : (n + 1) * HID] = slope
            act = act.astype(bf16)
            if blk == 0:
                u_ref[...] = act
            elif blk == 2:
                act = act.astype(f32) * (0.5 * DH**-0.5)
                qt_ref[...] = act.T.astype(bf16)
                for hp, part in enumerate(pairs_of(act.astype(bf16))):
                    q_ref[hp] = part
            else:
                target, turned = (v_ref, vt_ref) if blk == 1 else (k_ref, kt_ref)
                turned[half] = act.T
                for hp, part in enumerate(pairs_of(act)):
                    target[half, hp] = part

    def plus(a, b):
        return b if a is None else a + b

    def forward(hp, lower):
        q, k = q_ref[hp], k_ref[1, hp]
        if lower:
            kl = k_ref[0, hp]
        row = lax.broadcasted_iota(jnp.int32, (QB, 1), 0)
        for h in range(2):
            head = 2 * hp + h
            hs = pl.ds(pl.multiple_of(head * DH, DH), DH)
            vt = vt_ref[1, hs, :]
            qm = q * head_mask[h]
            att = [None, None]
            for qi in range(2):
                for ki in range(qi + 1):
                    act, slope = gate(dot_nt(qm[parts[qi]], k[parts[ki]]))
                    if ki == qi:
                        limit = jnp.minimum(row, length - 1 - base - ki * QB)
                        ok = lax.broadcasted_iota(jnp.int32, act.shape, 1) <= limit
                        act = jnp.where(ok, act, 0.0)
                        slope = jnp.where(ok, slope, 0.0)
                    at = 2 * qi + ki
                    p = act.astype(bf16)
                    p_ref[head, at] = p
                    d_ref[head, at] = slope
                    att[qi] = plus(att[qi], dot_nt(vt[:, parts[ki]], p))
                if lower:
                    act, slope = gate(dot_nt(qm[parts[qi]], kl))
                    p = act.astype(bf16)
                    pl_ref[head, parts[qi]] = p
                    dl_ref[head, parts[qi]] = slope
                    att[qi] = att[qi] + dot_nt(vt_ref[0, hs, :], p)
            att_ref[hs, :] = jnp.concatenate(att, axis=1)

    def backward(hp, lower):
        v, do = v_ref[1, hp], do_ref[hp]
        if lower:
            vl = v_ref[0, hp]
        for h in range(2):
            head = 2 * hp + h
            hs = pl.ds(pl.multiple_of(head * DH, DH), DH)
            qt = qt_ref[hs, :]
            dot = dot_ref[hs, :]
            kt = kt_ref[1, hs, :]
            dm = do * head_mask[h]
            dq = [None, None]
            dk = [None, None]
            dv = [None, None]
            if lower:
                dkl, dvl = None, None
            for qi in range(2):
                qs = parts[qi]
                for ki in range(qi + 1):
                    at = 2 * qi + ki
                    ds = (dot_nt(dm[qs], v[parts[ki]]) * d_ref[head, at]).astype(bf16)
                    dq[qi] = plus(dq[qi], dot_nt(kt[:, parts[ki]], ds))
                    dk[ki] = plus(dk[ki], dot_nn(qt[:, qs], ds))
                    dv[ki] = plus(dv[ki], dot_nn(dot[:, qs], p_ref[head, at]))
                if lower:
                    ds = (dot_nt(dm[qs], vl) * dl_ref[head, qs]).astype(bf16)
                    dq[qi] = plus(dq[qi], dot_nt(kt_ref[0, hs, :], ds))
                    dkl = plus(dkl, dot_nn(qt[:, qs], ds))
                    dvl = plus(dvl, dot_nn(dot[:, qs], pl_ref[head, qs]))
            att_ref[hs, :] = jnp.concatenate(dq, axis=1)
            dk_ref[hs, :] = jnp.concatenate(dk, axis=1)
            dv_ref[hs, :] = jnp.concatenate(dv, axis=1)
            if lower:
                dkl_ref[hs, :] = dkl
                dvl_ref[hs, :] = dvl

    def over_pairs(body):
        @pl.when(upper)
        def _():
            @pl.loop(0, PAIRS)
            def _(hp):
                body(hp, True)

        @pl.when(jnp.logical_not(upper))
        def _():
            @pl.loop(0, PAIRS)
            def _(hp):
                body(hp, False)

    g_ref[...] = jnp.zeros_like(g_ref)

    @pl.when(jnp.logical_not(active))
    def _():
        for load in loads:
            load.wait()
        out_ref[...] = jnp.zeros_like(out_ref)

    @pl.when(active)
    def _():
        x = features(seq)
        for load in loads:
            load.wait()
        x_ref[...] = x
        y, r = norm(x)
        y_ref[...] = y
        r_ref[...] = 0.5 * r
        project(1, (0, 1, 2, 3), (0.5 * y).astype(bf16), slope_ref)

        @pl.when(upper)
        def _():
            y, r = norm(features(0))
            yl_ref[...] = y
            rl_ref[...] = 0.5 * r
            project(0, (1, 3), (0.5 * y).astype(bf16), slopel_ref)

        over_pairs(forward)

        na, ra = norm(att_ref[...].T * (1.0 / LEN))
        u = u_ref[...].astype(f32)
        valid = (base + lax.broadcasted_iota(jnp.int32, (HALF, 1), 0)) < length
        mixed = dot_nn((na * u).astype(bf16), wo_ref[...]) + x_ref[...]
        out_ref[...] = jnp.where(valid, mixed, 0.0).astype(bf16)
        cot = jnp.where(valid, cot_ref[...].astype(f32), 0.0)
        gg = dot_nt(cot.astype(bf16), wo_ref[...])
        pg_ref[:, :HID] = (gg * na * slope_ref[:, :HID]).astype(bf16)
        da = norm_back(na, ra * (1.0 / LEN), gg * u)
        dot_ref[...] = da.T.astype(bf16)
        for hp, part in enumerate(pairs_of(da.astype(bf16))):
            do_ref[hp] = part

        over_pairs(backward)

        dq = att_ref[...].T * (0.5 * DH**-0.5)
        pg_ref[:, HID : 2 * HID] = (dv_ref[...].T * slope_ref[:, HID : 2 * HID]).astype(bf16)
        pg_ref[:, 2 * HID : 3 * HID] = (dq * slope_ref[:, 2 * HID : 3 * HID]).astype(bf16)
        pg_ref[:, 3 * HID :] = (dk_ref[...].T * slope_ref[:, 3 * HID :]).astype(bf16)
        eg = dot_nt(pg_ref[...], w_ref[...])
        cot = jnp.where(valid, cot_ref[...].astype(f32), 0.0)
        put_grad(seq, cot + norm_back(y_ref[...], r_ref[...], eg))

        @pl.when(upper)
        def _():
            pgl_ref[:, :HID] = (dvl_ref[...].T * slopel_ref[:, :HID]).astype(bf16)
            pgl_ref[:, HID:] = (dkl_ref[...].T * slopel_ref[:, HID:]).astype(bf16)
            eg = dot_nt(pgl_ref[:, :HID], w_ref[:, HID : 2 * HID])
            eg = eg + dot_nt(pgl_ref[:, HID:], w_ref[:, 3 * HID :])
            put_grad(0, norm_back(yl_ref[...], rl_ref[...], eg))


def vmem():
    return pl.BlockSpec(memory_space=pltpu.VMEM)


def hbm():
    return pl.BlockSpec(memory_space=pl.ANY)


def smem():
    return pl.BlockSpec(memory_space=pltpu.SMEM)


def in_vmem(x):
    return pltpu.with_memory_space_constraint(x, pltpu.VMEM)


def params():
    return pltpu.CompilerParams(vmem_limit_bytes=60 * 1024 * 1024)


def table_rows(table):
    return pl.pallas_call(
        rows_kernel,
        in_specs=[vmem()],
        out_specs=vmem(),
        out_shape=pltpu.VMEM((G_HI, BLK), f32),
        compiler_params=params(),
        name="table_rows",
    )(table)


def gather(seq, lengths, own, other, rows):
    return pl.pallas_call(
        gather_kernel,
        in_specs=[smem(), smem(), vmem(), vmem(), vmem()],
        out_specs=vmem(),
        out_shape=jax.ShapeDtypeStruct((USERS, 2, FEAT, HALF), bf16),
        scratch_shapes=[
            pltpu.VMEM((2, NBLK, USERS, BLK), jnp.int32),
            pltpu.VMEM((2, G_STEP, BLK), jnp.int32),
            pltpu.VMEM((2, G_STEP * BLK, BLK), f32),
            pltpu.SMEM((USERS * NBLK + NBLK,), jnp.int32),
            pltpu.SMEM((2, G_STEP, BLK), jnp.int32),
            pltpu.SemaphoreType.DMA((2,)),
        ],
        compiler_params=params(),
        name="gather",
    )(seq, lengths, own, other, rows)


def scatter(seq, lengths, half, own, other, grad, dtype):
    return pl.pallas_call(
        scatter_kernel,
        in_specs=[smem(), smem(), smem(), vmem(), vmem(), vmem()],
        out_specs=vmem(),
        out_shape=jax.ShapeDtypeStruct((FEAT, S_ROWS), dtype),
        scratch_shapes=[
            pltpu.VMEM((2, NBLK, USERS, BLK), jnp.int32),
            pltpu.VMEM((S_LO * FEAT, S_HI), f32),
            pltpu.SMEM((USERS * NBLK + NBLK,), jnp.int32),
        ],
        compiler_params=params(),
        name="scatter",
    )(seq, lengths, half, own, other, grad)


def layer(seq, col, lengths, e, w, wo, cot):
    return pl.pallas_call(
        layer_kernel,
        in_specs=[smem(), smem(), smem(), vmem(), hbm(), hbm(), hbm()],
        out_specs=(vmem(), vmem()),
        out_shape=(
            jax.ShapeDtypeStruct((HALF, D), bf16),
            jax.ShapeDtypeStruct((USERS, 2, FEAT, HALF), bf16),
        ),
        scratch_shapes=[
            pltpu.VMEM((D, 4 * HID), bf16),
            pltpu.VMEM((HID, D), bf16),
            pltpu.VMEM((HALF, D), bf16),
            pltpu.SemaphoreType.DMA((3,)),
            pltpu.VMEM((HALF, D), f32),
            pltpu.VMEM((HALF, D), f32),
            pltpu.VMEM((HALF, 1), f32),
            pltpu.VMEM((HALF, D), f32),
            pltpu.VMEM((HALF, 1), f32),
            pltpu.VMEM((HALF, 4 * HID), f32),
            pltpu.VMEM((HALF, 2 * HID), f32),
            pltpu.VMEM((HALF, HID), bf16),
            pltpu.VMEM((PAIRS, HALF, 2 * DH), bf16),
            pltpu.VMEM((HID, HALF), bf16),
            pltpu.VMEM((2, PAIRS, HALF, 2 * DH), bf16),
            pltpu.VMEM((2, HID, HALF), bf16),
            pltpu.VMEM((2, PAIRS, HALF, 2 * DH), bf16),
            pltpu.VMEM((2, HID, HALF), bf16),
            pltpu.VMEM((H, 4, HALF // 2, HALF // 2), bf16),
            pltpu.VMEM((H, 4, HALF // 2, HALF // 2), f32),
            pltpu.VMEM((H, HALF, HALF), bf16),
            pltpu.VMEM((H, HALF, HALF), f32),
            pltpu.VMEM((HID, HALF), f32),
            pltpu.VMEM((PAIRS, HALF, 2 * DH), bf16),
            pltpu.VMEM((HID, HALF), bf16),
            pltpu.VMEM((HID, HALF), f32),
            pltpu.VMEM((HID, HALF), f32),
            pltpu.VMEM((HID, HALF), f32),
            pltpu.VMEM((HID, HALF), f32),
            pltpu.VMEM((HALF, 4 * HID), bf16),
            pltpu.VMEM((HALF, 2 * HID), bf16),
        ],
        compiler_params=params(),
        name="layer",
    )(seq, col, lengths, e, w, wo, cot)


def per_device(history_items, lengths, item_table, input_weight, output_weight, output_cotangent):
    col = lax.axis_index("col").astype(jnp.int32).reshape(1)
    seq = lax.axis_index("seq").astype(jnp.int32).reshape(1)
    swap = [(0, 1), (1, 0)]
    both = ("col", "seq")
    own = history_items
    other = in_vmem(lax.ppermute(own, "seq", swap))
    rows = in_vmem(table_rows(item_table))
    looked = gather(seq, lengths, own, other, rows)
    flat = looked.reshape(2 * USERS, FEAT, HALF)
    arrived = lax.all_to_all(flat, both, split_axis=0, concat_axis=0, tiled=True)
    arrived = in_vmem(arrived.reshape(USERS, 2, FEAT, HALF))
    out, grad = layer(
        seq, col, lengths, arrived, input_weight, output_weight, output_cotangent[0]
    )
    grad = grad.reshape(2 * USERS, FEAT, HALF)
    back = lax.all_to_all(grad, both, split_axis=0, concat_axis=0, tiled=True)
    back = in_vmem(back.reshape(USERS, 2, FEAT, HALF))
    theirs = scatter(seq, lengths, 1 - seq, own, other, back, bf16)
    received = lax.ppermute(theirs, "seq", swap)
    mine = scatter(seq, lengths, seq, own, other, back, f32)
    return (out[None], mine + received.astype(f32))


def solution(mesh):
    in_specs = (P(None, "seq"), P(), P("col", None), P(), P(), P("col", "seq", None))
    out_specs = (P("col", "seq", None), P("col", "seq"))
    return jax.shard_map(
        per_device, mesh=mesh, in_specs=in_specs, out_specs=out_specs, check_vma=False
    )
```

```python
import jax
import jax.numpy as jnp
from jax import lax
from jax.experimental import pallas as pl
from jax.experimental.pallas import tpu as pltpu
from jax.sharding import PartitionSpec as P

H = 8
DH = 64
LEN = 1024
D = 512
HID = H * DH
USERS = 64
FEAT = 8
HALF = 512
BLK = 128
NBLK = HALF // BLK
ROWS = 65536
PAIRS = H // 2
norm_epsilon = 1e-05
bf16 = jnp.bfloat16
f32 = jnp.float32

G_LO = 16
G_HI = ROWS // G_LO
G_STEP = 8
S_ROWS = ROWS // 2
S_LO = 32
S_HI = S_ROWS // S_LO
S_STEP = 16


def block_list(seq, lengths_ref, list_ref):
    def step(u, count):
        parity = (seq + u) & 1
        blocks = (lengths_ref[u] + (BLK - 1)) >> 7
        for i in range(NBLK):
            list_ref[count + i] = u * NBLK + i
        return count + ((blocks + 1 - parity) >> 1)

    return lax.fori_loop(0, USERS, step, 0)


def item_row(items_ref, seq, block):
    u = block >> 2
    i = block & 3
    parity = (seq + u) & 1
    return items_ref[i >> 1, 2 * (i & 1) + parity, pl.ds(u, 1), :]


def stage_items(seq, own_ref, other_ref, items_ref):
    for b in range(NBLK):
        items_ref[seq, b] = own_ref[:, b * BLK : (b + 1) * BLK]
        items_ref[1 - seq, b] = other_ref[:, b * BLK : (b + 1) * BLK]


def onehot(index, rows):
    n = index.shape[1]
    iota = lax.broadcasted_iota(jnp.int16, (rows, n), 0)
    wide = jnp.broadcast_to(index.astype(jnp.int16), (rows, n))
    return jnp.where(iota == wide, jnp.ones((), bf16), jnp.zeros((), bf16))


def rows_kernel(table_ref, rows_ref):
    step = 512
    for c in range(G_HI // step):
        parts = [
            table_ref[:, lo * G_HI + c * step : lo * G_HI + (c + 1) * step] for lo in range(G_LO)
        ]
        rows_ref[c * step : (c + 1) * step, :] = jnp.concatenate(parts, axis=0).T


def gather_kernel(
    seq_ref, lengths_ref, own_ref, other_ref, rows_ref, out_ref,
    items_ref, stage_ref, got_ref, list_ref, index_ref, sems,
):
    seq = seq_ref[0]
    stage_items(seq, own_ref, other_ref, items_ref)
    out_ref[...] = jnp.zeros_like(out_ref)
    count = block_list(seq, lengths_ref, list_ref)
    pairs = (count + 2 * G_STEP - 1) // (2 * G_STEP)

    def ids_of(g):
        last = count - 1
        return [list_ref[jnp.minimum(g * G_STEP + j, last)] for j in range(G_STEP)]

    def copy(slot):
        return pltpu.make_async_copy(stage_ref.at[slot], index_ref.at[slot], sems.at[slot])

    def fetch(g, slot):
        rows = jnp.concatenate([item_row(items_ref, seq, b) for b in ids_of(g)], axis=0)
        stage_ref[slot] = rows & (G_HI - 1)
        copy(slot).start()

    def move(slot):
        for j in range(G_STEP):
            for t in range(BLK):
                r = index_ref[slot, j, t]
                got_ref[slot, pl.ds(j * BLK + t, 1), :] = rows_ref[pl.ds(r, 1), :]

    def finish(g, slot):
        ids = ids_of(g)
        for j in range(G_STEP):
            u = ids[j] >> 2
            col = pl.multiple_of((ids[j] & 3) * BLK, BLK)
            lo = lax.shift_right_logical(item_row(items_ref, seq, ids[j]), 12)
            part = got_ref[slot, j * BLK : (j + 1) * BLK, :].T.reshape(G_LO, FEAT, BLK)
            mask = lax.broadcasted_iota(jnp.int32, (G_LO, FEAT, BLK), 0) == lo.reshape(1, 1, BLK)
            part = jnp.sum(jnp.where(mask, part, 0.0), axis=0).astype(bf16)
            out_ref[u, 0, :, pl.ds(col, BLK)] = part
            out_ref[u, 1, :, pl.ds(col, BLK)] = part

    got_ref[1] = jnp.zeros_like(got_ref[1])
    for slot in range(2):
        fetch(slot, slot)

    def step(p, carry):
        for slot in range(2):
            g = 2 * p + slot
            copy(slot).wait()
            move(slot)
            finish(jnp.maximum(g - 1, 0), 1 - slot)
            fetch(g + 2, slot)
        return carry

    lax.fori_loop(0, pairs, step, 0)
    finish(2 * pairs - 1, 1)
    for slot in range(2):
        copy(slot).wait()


def scatter_kernel(
    seq_ref, lengths_ref, half_ref, own_ref, other_ref, grad_ref, out_ref, items_ref, acc_ref, list_ref
):
    seq = seq_ref[0]
    base = half_ref[0] * S_ROWS
    stage_items(seq, own_ref, other_ref, items_ref)
    acc_ref[...] = jnp.zeros_like(acc_ref)
    count = block_list(seq, lengths_ref, list_ref)

    def step(g, carry):
        rows, grads = [], []
        for j in range(S_STEP):
            at = g * S_STEP + j
            b = list_ref[jnp.maximum(jnp.minimum(at, count - 1), 0)]
            row = item_row(items_ref, seq, b) - base
            rows.append(jnp.where(at < count, row, -1))
            u = b >> 2
            col = pl.multiple_of((b & 3) * BLK, BLK)
            grads.append(
                grad_ref[u, 0, :, pl.ds(col, BLK)].astype(f32)
                + grad_ref[u, 1, :, pl.ds(col, BLK)].astype(f32)
            )
        index = jnp.concatenate(rows, axis=1)
        grad = jnp.concatenate(grads, axis=1)
        n = S_STEP * BLK
        lo = lax.shift_right_arithmetic(index, 10)
        hi = index & (S_HI - 1)
        mask = lax.broadcasted_iota(jnp.int32, (S_LO, FEAT, n), 0) == lo.reshape(1, 1, n)
        spread = jnp.where(mask, jnp.broadcast_to(grad[None], (S_LO, FEAT, n)), 0.0)
        spread = spread.reshape(S_LO * FEAT, n).astype(bf16)
        acc_ref[...] += lax.dot_general(
            spread, onehot(hi, S_HI), (((1,), (1,)), ((), ())), preferred_element_type=f32
        )
        return carry

    lax.fori_loop(0, (count + S_STEP - 1) // S_STEP, step, 0)
    for lo in range(S_LO):
        out_ref[:, lo * S_HI : (lo + 1) * S_HI] = acc_ref[lo * FEAT : (lo + 1) * FEAT, :].astype(
            out_ref.dtype
        )


def dot_nt(a, b):
    return lax.dot_general(a, b, (((1,), (1,)), ((), ())), preferred_element_type=f32)


def dot_nn(a, b):
    return jnp.dot(a, b, preferred_element_type=f32)


def norm(z):
    m = jnp.mean(z, axis=-1, keepdims=True)
    c = z - m
    w = jnp.mean(c * c, axis=-1, keepdims=True)
    r = lax.rsqrt(w + norm_epsilon)
    return c * r, r


def norm_back(y, r, dy):
    a = jnp.mean(dy, axis=-1, keepdims=True)
    b = jnp.mean(dy * y, axis=-1, keepdims=True)
    return r * (dy - a - y * b)


def gate(h):
    t = jnp.tanh(h)
    a = 1.0 + t
    act = h * a
    return act, a + act * (1.0 - t)


def slope_of(a, p):
    return a + p.astype(f32) * (2.0 - a)


def layer_kernel(
    seq_ref, col_ref, lengths_ref, e_ref, w_hbm, wo_hbm, cot_hbm, out_ref, g_ref,
    w_ref, wo_ref, cot_ref, sems,
    x_ref, y_ref, r_ref, yl_ref, rl_ref, slope_ref, slopel_ref, u_ref, q_ref, qt_ref, k_ref, kt_ref, v_ref, vt_ref,
    p_ref, d_ref, pl_ref, dl_ref, att_ref, do_ref, dot_ref, dk_ref, dv_ref, dkl_ref, dvl_ref,
    pg_ref, pgl_ref,
):
    seq = seq_ref[0]
    col = col_ref[0]
    length = lengths_ref[col]
    base = seq * HALF
    upper = seq == 1
    active = length > base
    lanes = lax.broadcasted_iota(jnp.int32, (1, 2 * DH), 1)
    head_mask = [(lanes < DH).astype(f32).astype(bf16), (lanes >= DH).astype(f32).astype(bf16)]
    loads = [
        pltpu.make_async_copy(src, dst, sems.at[n])
        for n, (src, dst) in enumerate(((w_hbm, w_ref), (wo_hbm, wo_ref), (cot_hbm, cot_ref)))
    ]
    for load in loads:
        load.start()
    QB = HALF // 2
    parts = [slice(0, QB), slice(QB, HALF)]

    def place(half, b):
        i = 2 * half + b // 2
        return (b + col) & 1, pl.multiple_of(i * BLK, BLK)

    def features(half):
        parts = []
        for b in range(NBLK):
            src, at = place(half, b)
            part = e_ref[:, src, :, pl.ds(at, BLK)].astype(f32).reshape(D, BLK)
            parts.append(part.T)
        return jnp.concatenate(parts, axis=0)

    def put_grad(half, grad):
        flat = grad.T.reshape(D // FEAT, FEAT, HALF).astype(bf16)
        for b in range(NBLK):
            dst, at = place(half, b)
            g_ref[:, dst, :, pl.ds(at, BLK)] = flat[:, :, b * BLK : (b + 1) * BLK]

    def pairs_of(act):
        return [act[:, hp * 2 * DH : (hp + 1) * 2 * DH] for hp in range(PAIRS)]

    def project(half, blocks, yb, slopes):
        for n, blk in enumerate(blocks):
            act, slope = gate(dot_nn(yb, w_ref[:, blk * HID : (blk + 1) * HID]))
            slopes[:, n * HID : (n + 1) * HID] = slope
            act = act.astype(bf16)
            if blk == 0:
                u_ref[...] = act
            elif blk == 2:
                act = act.astype(f32) * (0.5 * DH**-0.5)
                qt_ref[...] = act.T.astype(bf16)
                for hp, part in enumerate(pairs_of(act.astype(bf16))):
                    q_ref[hp] = part
            else:
                target, turned = (v_ref, vt_ref) if blk == 1 else (k_ref, kt_ref)
                turned[half] = act.T
                for hp, part in enumerate(pairs_of(act)):
                    target[half, hp] = part

    def plus(a, b):
        return b if a is None else a + b

    def forward(hp, lower):
        q, k = q_ref[hp], k_ref[1, hp]
        if lower:
            kl = k_ref[0, hp]
        row = lax.broadcasted_iota(jnp.int32, (QB, 1), 0)
        for h in range(2):
            head = 2 * hp + h
            hs = pl.ds(pl.multiple_of(head * DH, DH), DH)
            vt = vt_ref[1, hs, :]
            qm = q * head_mask[h]
            att = [None, None]
            for qi in range(2):
                for ki in range(qi + 1):
                    half = dot_nt(qm[parts[qi]], k[parts[ki]])
                    a = 1.0 + jnp.tanh(half)
                    if ki == qi:
                        limit = jnp.minimum(row, length - 1 - base - ki * QB)
                        ok = lax.broadcasted_iota(jnp.int32, a.shape, 1) <= limit
                        a = jnp.where(ok, a, 0.0)
                    at = 2 * qi + ki
                    p = (half * a).astype(bf16)
                    p_ref[head, at] = p
                    d_ref[head, at] = a
                    att[qi] = plus(att[qi], dot_nt(vt[:, parts[ki]], p))
                if lower:
                    half = dot_nt(qm[parts[qi]], kl)
                    a = 1.0 + jnp.tanh(half)
                    p = (half * a).astype(bf16)
                    pl_ref[head, parts[qi]] = p
                    dl_ref[head, parts[qi]] = a
                    att[qi] = att[qi] + dot_nt(vt_ref[0, hs, :], p)
            att_ref[hs, :] = jnp.concatenate(att, axis=1)

    def backward(hp, lower):
        v, do = v_ref[1, hp], do_ref[hp]
        if lower:
            vl = v_ref[0, hp]
        for h in range(2):
            head = 2 * hp + h
            hs = pl.ds(pl.multiple_of(head * DH, DH), DH)
            qt = qt_ref[hs, :]
            dot = dot_ref[hs, :]
            kt = kt_ref[1, hs, :]
            dm = do * head_mask[h]
            dq = [None, None]
            dk = [None, None]
            dv = [None, None]
            if lower:
                dkl, dvl = None, None
            for qi in range(2):
                qs = parts[qi]
                for ki in range(qi + 1):
                    at = 2 * qi + ki
                    p = p_ref[head, at]
                    ds = (dot_nt(dm[qs], v[parts[ki]]) * slope_of(d_ref[head, at], p)).astype(bf16)
                    dq[qi] = plus(dq[qi], dot_nt(kt[:, parts[ki]], ds))
                    dk[ki] = plus(dk[ki], dot_nn(qt[:, qs], ds))
                    dv[ki] = plus(dv[ki], dot_nn(dot[:, qs], p))
                if lower:
                    p = pl_ref[head, qs]
                    ds = (dot_nt(dm[qs], vl) * slope_of(dl_ref[head, qs], p)).astype(bf16)
                    dq[qi] = plus(dq[qi], dot_nt(kt_ref[0, hs, :], ds))
                    dkl = plus(dkl, dot_nn(qt[:, qs], ds))
                    dvl = plus(dvl, dot_nn(dot[:, qs], p))
            att_ref[hs, :] = jnp.concatenate(dq, axis=1)
            dk_ref[hs, :] = jnp.concatenate(dk, axis=1)
            dv_ref[hs, :] = jnp.concatenate(dv, axis=1)
            if lower:
                dkl_ref[hs, :] = dkl
                dvl_ref[hs, :] = dvl

    def over_pairs(body):
        @pl.when(upper)
        def _():
            @pl.loop(0, PAIRS)
            def _(hp):
                body(hp, True)

        @pl.when(jnp.logical_not(upper))
        def _():
            @pl.loop(0, PAIRS)
            def _(hp):
                body(hp, False)

    g_ref[...] = jnp.zeros_like(g_ref)

    @pl.when(jnp.logical_not(active))
    def _():
        for load in loads:
            load.wait()
        out_ref[...] = jnp.zeros_like(out_ref)

    @pl.when(active)
    def _():
        x = features(seq)
        for load in loads:
            load.wait()
        x_ref[...] = x
        y, r = norm(x)
        y_ref[...] = y
        r_ref[...] = 0.5 * r
        project(1, (0, 1, 2, 3), (0.5 * y).astype(bf16), slope_ref)

        @pl.when(upper)
        def _():
            y, r = norm(features(0))
            yl_ref[...] = y
            rl_ref[...] = 0.5 * r
            project(0, (1, 3), (0.5 * y).astype(bf16), slopel_ref)

        over_pairs(forward)

        na, ra = norm(att_ref[...].T * (1.0 / LEN))
        u = u_ref[...].astype(f32)
        valid = (base + lax.broadcasted_iota(jnp.int32, (HALF, 1), 0)) < length
        mixed = dot_nn((na * u).astype(bf16), wo_ref[...]) + x_ref[...]
        out_ref[...] = jnp.where(valid, mixed, 0.0).astype(bf16)
        cot = jnp.where(valid, cot_ref[...].astype(f32), 0.0)
        gg = dot_nt(cot.astype(bf16), wo_ref[...])
        pg_ref[:, :HID] = (gg * na * slope_ref[:, :HID]).astype(bf16)
        da = norm_back(na, ra * (1.0 / LEN), gg * u)
        dot_ref[...] = da.T.astype(bf16)
        for hp, part in enumerate(pairs_of(da.astype(bf16))):
            do_ref[hp] = part

        over_pairs(backward)

        dq = att_ref[...].T * (0.5 * DH**-0.5)
        pg_ref[:, HID : 2 * HID] = (dv_ref[...].T * slope_ref[:, HID : 2 * HID]).astype(bf16)
        pg_ref[:, 2 * HID : 3 * HID] = (dq * slope_ref[:, 2 * HID : 3 * HID]).astype(bf16)
        pg_ref[:, 3 * HID :] = (dk_ref[...].T * slope_ref[:, 3 * HID :]).astype(bf16)
        eg = dot_nt(pg_ref[...], w_ref[...])
        cot = jnp.where(valid, cot_ref[...].astype(f32), 0.0)
        put_grad(seq, cot + norm_back(y_ref[...], r_ref[...], eg))

        @pl.when(upper)
        def _():
            pgl_ref[:, :HID] = (dvl_ref[...].T * slopel_ref[:, :HID]).astype(bf16)
            pgl_ref[:, HID:] = (dkl_ref[...].T * slopel_ref[:, HID:]).astype(bf16)
            eg = dot_nt(pgl_ref[:, :HID], w_ref[:, HID : 2 * HID])
            eg = eg + dot_nt(pgl_ref[:, HID:], w_ref[:, 3 * HID :])
            put_grad(0, norm_back(yl_ref[...], rl_ref[...], eg))


def vmem():
    return pl.BlockSpec(memory_space=pltpu.VMEM)


def hbm():
    return pl.BlockSpec(memory_space=pl.ANY)


def smem():
    return pl.BlockSpec(memory_space=pltpu.SMEM)


def in_vmem(x):
    return pltpu.with_memory_space_constraint(x, pltpu.VMEM)


def params():
    return pltpu.CompilerParams(vmem_limit_bytes=60 * 1024 * 1024)


def table_rows(table):
    return pl.pallas_call(
        rows_kernel,
        in_specs=[vmem()],
        out_specs=vmem(),
        out_shape=pltpu.VMEM((G_HI, BLK), f32),
        compiler_params=params(),
        name="table_rows",
    )(table)


def gather(seq, lengths, own, other, rows):
    return pl.pallas_call(
        gather_kernel,
        in_specs=[smem(), smem(), vmem(), vmem(), vmem()],
        out_specs=vmem(),
        out_shape=pltpu.VMEM((USERS, 2, FEAT, HALF), bf16),
        scratch_shapes=[
            pltpu.VMEM((2, NBLK, USERS, BLK), jnp.int32),
            pltpu.VMEM((2, G_STEP, BLK), jnp.int32),
            pltpu.VMEM((2, G_STEP * BLK, BLK), f32),
            pltpu.SMEM((USERS * NBLK + NBLK,), jnp.int32),
            pltpu.SMEM((2, G_STEP, BLK), jnp.int32),
            pltpu.SemaphoreType.DMA((2,)),
        ],
        compiler_params=params(),
        name="gather",
    )(seq, lengths, own, other, rows)


def scatter(seq, lengths, half, own, other, grad, dtype):
    return pl.pallas_call(
        scatter_kernel,
        in_specs=[smem(), smem(), smem(), vmem(), vmem(), vmem()],
        out_specs=vmem(),
        out_shape=pltpu.VMEM((FEAT, S_ROWS), dtype),
        scratch_shapes=[
            pltpu.VMEM((2, NBLK, USERS, BLK), jnp.int32),
            pltpu.VMEM((S_LO * FEAT, S_HI), f32),
            pltpu.SMEM((USERS * NBLK + NBLK,), jnp.int32),
        ],
        compiler_params=params(),
        name="scatter",
    )(seq, lengths, half, own, other, grad)


def layer(seq, col, lengths, e, w, wo, cot):
    return pl.pallas_call(
        layer_kernel,
        in_specs=[smem(), smem(), smem(), vmem(), hbm(), hbm(), hbm()],
        out_specs=(vmem(), vmem()),
        out_shape=(
            jax.ShapeDtypeStruct((HALF, D), bf16),
            pltpu.VMEM((USERS, 2, FEAT, HALF), bf16),
        ),
        scratch_shapes=[
            pltpu.VMEM((D, 4 * HID), bf16),
            pltpu.VMEM((HID, D), bf16),
            pltpu.VMEM((HALF, D), bf16),
            pltpu.SemaphoreType.DMA((3,)),
            pltpu.VMEM((HALF, D), f32),
            pltpu.VMEM((HALF, D), f32),
            pltpu.VMEM((HALF, 1), f32),
            pltpu.VMEM((HALF, D), f32),
            pltpu.VMEM((HALF, 1), f32),
            pltpu.VMEM((HALF, 4 * HID), f32),
            pltpu.VMEM((HALF, 2 * HID), f32),
            pltpu.VMEM((HALF, HID), bf16),
            pltpu.VMEM((PAIRS, HALF, 2 * DH), bf16),
            pltpu.VMEM((HID, HALF), bf16),
            pltpu.VMEM((2, PAIRS, HALF, 2 * DH), bf16),
            pltpu.VMEM((2, HID, HALF), bf16),
            pltpu.VMEM((2, PAIRS, HALF, 2 * DH), bf16),
            pltpu.VMEM((2, HID, HALF), bf16),
            pltpu.VMEM((H, 4, HALF // 2, HALF // 2), bf16),
            pltpu.VMEM((H, 4, HALF // 2, HALF // 2), f32),
            pltpu.VMEM((H, HALF, HALF), bf16),
            pltpu.VMEM((H, HALF, HALF), f32),
            pltpu.VMEM((HID, HALF), f32),
            pltpu.VMEM((PAIRS, HALF, 2 * DH), bf16),
            pltpu.VMEM((HID, HALF), bf16),
            pltpu.VMEM((HID, HALF), f32),
            pltpu.VMEM((HID, HALF), f32),
            pltpu.VMEM((HID, HALF), f32),
            pltpu.VMEM((HID, HALF), f32),
            pltpu.VMEM((HALF, 4 * HID), bf16),
            pltpu.VMEM((HALF, 2 * HID), bf16),
        ],
        compiler_params=params(),
        name="layer",
    )(seq, col, lengths, e, w, wo, cot)


def per_device(history_items, lengths, item_table, input_weight, output_weight, output_cotangent):
    col = lax.axis_index("col").astype(jnp.int32).reshape(1)
    seq = lax.axis_index("seq").astype(jnp.int32).reshape(1)
    swap = [(0, 1), (1, 0)]
    both = ("col", "seq")
    own = history_items
    other = in_vmem(lax.ppermute(own, "seq", swap))
    rows = in_vmem(table_rows(item_table))
    looked = gather(seq, lengths, own, other, rows)
    flat = looked.reshape(2 * USERS, FEAT, HALF)
    arrived = lax.all_to_all(flat, both, split_axis=0, concat_axis=0, tiled=True)
    arrived = in_vmem(arrived.reshape(USERS, 2, FEAT, HALF))
    out, grad = layer(
        seq, col, lengths, arrived, input_weight, output_weight, output_cotangent[0]
    )
    grad = grad.reshape(2 * USERS, FEAT, HALF)
    back = lax.all_to_all(grad, both, split_axis=0, concat_axis=0, tiled=True)
    back = in_vmem(back.reshape(USERS, 2, FEAT, HALF))
    theirs = scatter(seq, lengths, 1 - seq, own, other, back, bf16)
    received = lax.ppermute(theirs, "seq", swap)
    mine = scatter(seq, lengths, seq, own, other, back, f32)
    return (out[None], mine + received.astype(f32))


def solution(mesh):
    in_specs = (P(None, "seq"), P(), P("col", None), P(), P(), P("col", "seq", None))
    out_specs = (P("col", "seq", None), P("col", "seq"))
    return jax.shard_map(
        per_device, mesh=mesh, in_specs=in_specs, out_specs=out_specs, check_vma=False
    )
```

```python
import jax
import jax.numpy as jnp
from jax import lax
from jax.experimental import pallas as pl
from jax.experimental.pallas import tpu as pltpu
from jax.sharding import PartitionSpec as P

H = 8
DH = 64
LEN = 1024
D = 512
HID = H * DH
USERS = 64
FEAT = 8
HALF = 512
BLK = 128
NBLK = HALF // BLK
ROWS = 65536
PAIRS = H // 2
AHEAD = 2
norm_epsilon = 1e-05
bf16 = jnp.bfloat16
f32 = jnp.float32

G_LO = 16
G_HI = ROWS // G_LO
G_STEP = 8
S_ROWS = ROWS // 2
S_LO = 32
S_HI = S_ROWS // S_LO
S_STEP = 16
S_REST = 4


def block_list(seq, lengths_ref, list_ref):
    def step(u, count):
        parity = (seq + u) & 1
        blocks = (lengths_ref[u] + (BLK - 1)) >> 7
        for i in range(NBLK):
            list_ref[count + i] = u * NBLK + i
        return count + ((blocks + 1 - parity) >> 1)

    return lax.fori_loop(0, USERS, step, 0)


def item_row(items_ref, seq, block):
    u = block >> 2
    i = block & 3
    parity = (seq + u) & 1
    return items_ref[i >> 1, 2 * (i & 1) + parity, pl.ds(u, 1), :]


def stage_items(seq, own_ref, other_ref, items_ref):
    for b in range(NBLK):
        items_ref[seq, b] = own_ref[:, b * BLK : (b + 1) * BLK]
        items_ref[1 - seq, b] = other_ref[:, b * BLK : (b + 1) * BLK]


def onehot(index, rows):
    n = index.shape[1]
    iota = lax.broadcasted_iota(jnp.int16, (rows, n), 0)
    wide = jnp.broadcast_to(index.astype(jnp.int16), (rows, n))
    return jnp.where(iota == wide, jnp.ones((), bf16), jnp.zeros((), bf16))


def rows_kernel(table_ref, rows_ref):
    step = 512
    for c in range(G_HI // step):
        parts = [
            table_ref[:, lo * G_HI + c * step : lo * G_HI + (c + 1) * step] for lo in range(G_LO)
        ]
        rows_ref[c * step : (c + 1) * step, :] = jnp.concatenate(parts, axis=0).T


def gather_kernel(
    seq_ref, lengths_ref, own_ref, other_ref, rows_ref, out_ref,
    items_ref, stage_ref, got_ref, list_ref, index_ref, sems,
):
    seq = seq_ref[0]
    stage_items(seq, own_ref, other_ref, items_ref)
    out_ref[...] = jnp.zeros_like(out_ref)
    count = block_list(seq, lengths_ref, list_ref)
    pairs = (count + 2 * G_STEP - 1) // (2 * G_STEP)

    def ids_of(g):
        last = count - 1
        return [list_ref[jnp.minimum(g * G_STEP + j, last)] for j in range(G_STEP)]

    def copy(slot):
        return pltpu.make_async_copy(stage_ref.at[slot], index_ref.at[slot], sems.at[slot])

    def fetch(g, slot):
        rows = jnp.concatenate([item_row(items_ref, seq, b) for b in ids_of(g)], axis=0)
        stage_ref[slot] = rows & (G_HI - 1)
        copy(slot).start()

    def move(slot):
        for j in range(G_STEP):
            for t in range(BLK):
                r = index_ref[slot, j, t]
                got_ref[slot, pl.ds(j * BLK + t, 1), :] = rows_ref[pl.ds(r, 1), :]

    def finish(g, slot):
        ids = ids_of(g)
        for j in range(G_STEP):
            u = ids[j] >> 2
            col = pl.multiple_of((ids[j] & 3) * BLK, BLK)
            lo = lax.shift_right_logical(item_row(items_ref, seq, ids[j]), 12)
            part = got_ref[slot, j * BLK : (j + 1) * BLK, :].T.reshape(G_LO, FEAT, BLK)
            mask = lax.broadcasted_iota(jnp.int32, (G_LO, FEAT, BLK), 0) == lo.reshape(1, 1, BLK)
            part = jnp.sum(jnp.where(mask, part, 0.0), axis=0).astype(bf16)
            out_ref[u, 0, :, pl.ds(col, BLK)] = part
            out_ref[u, 1, :, pl.ds(col, BLK)] = part

    got_ref[1] = jnp.zeros_like(got_ref[1])
    for slot in range(2):
        fetch(slot, slot)

    def step(p, carry):
        for slot in range(2):
            g = 2 * p + slot
            copy(slot).wait()
            move(slot)
            finish(jnp.maximum(g - 1, 0), 1 - slot)
            fetch(g + 2, slot)
        return carry

    lax.fori_loop(0, pairs, step, 0)
    finish(2 * pairs - 1, 1)
    for slot in range(2):
        copy(slot).wait()


def scatter_kernel(
    seq_ref, lengths_ref, half_ref, own_ref, other_ref, grad_ref, out_ref, items_ref, acc_ref, list_ref
):
    seq = seq_ref[0]
    base = half_ref[0] * S_ROWS
    stage_items(seq, own_ref, other_ref, items_ref)
    acc_ref[...] = jnp.zeros_like(acc_ref)
    count = block_list(seq, lengths_ref, list_ref)

    def add(first, number):
        rows, grads = [], []
        for j in range(number):
            at = first + j
            b = list_ref[jnp.maximum(jnp.minimum(at, count - 1), 0)]
            row = item_row(items_ref, seq, b) - base
            rows.append(jnp.where(at < count, row, -1))
            u = b >> 2
            col = pl.multiple_of((b & 3) * BLK, BLK)
            grads.append(
                grad_ref[u, 0, :, pl.ds(col, BLK)].astype(f32)
                + grad_ref[u, 1, :, pl.ds(col, BLK)].astype(f32)
            )
        index = jnp.concatenate(rows, axis=1)
        grad = jnp.concatenate(grads, axis=1)
        n = number * BLK
        lo = lax.shift_right_arithmetic(index, 10)
        hi = index & (S_HI - 1)
        mask = lax.broadcasted_iota(jnp.int32, (S_LO, FEAT, n), 0) == lo.reshape(1, 1, n)
        spread = jnp.where(mask, jnp.broadcast_to(grad[None], (S_LO, FEAT, n)), 0.0)
        spread = spread.reshape(S_LO * FEAT, n).astype(bf16)
        acc_ref[...] += lax.dot_general(
            spread, onehot(hi, S_HI), (((1,), (1,)), ((), ())), preferred_element_type=f32
        )

    whole = lax.div(count, S_STEP)

    @pl.loop(0, whole)
    def _(g):
        add(g * S_STEP, S_STEP)

    @pl.loop(0, lax.div(count - whole * S_STEP + (S_REST - 1), S_REST))
    def _(g):
        add(whole * S_STEP + g * S_REST, S_REST)

    for lo in range(S_LO):
        out_ref[:, lo * S_HI : (lo + 1) * S_HI] = acc_ref[lo * FEAT : (lo + 1) * FEAT, :].astype(
            out_ref.dtype
        )


def dot_nt(a, b):
    return lax.dot_general(a, b, (((1,), (1,)), ((), ())), preferred_element_type=f32)


def dot_nn(a, b):
    return jnp.dot(a, b, preferred_element_type=f32)


def norm(z):
    m = jnp.mean(z, axis=-1, keepdims=True)
    c = z - m
    w = jnp.mean(c * c, axis=-1, keepdims=True)
    r = lax.rsqrt(w + norm_epsilon)
    return c * r, r


def norm_back(y, r, dy):
    a = jnp.mean(dy, axis=-1, keepdims=True)
    b = jnp.mean(dy * y, axis=-1, keepdims=True)
    return r * (dy - a - y * b)


def gate(h):
    t = jnp.tanh(h)
    a = 1.0 + t
    act = h * a
    return act, a + act * (1.0 - t)


def slope_of(a, p):
    return a + p.astype(f32) * (2.0 - a)


def layer_kernel(
    seq_ref, col_ref, lengths_ref, e_ref, w_hbm, wo_hbm, cot_hbm, out_ref, g_ref,
    w_ref, wo_ref, cot_ref, sems,
    x_ref, y_ref, r_ref, yl_ref, rl_ref, slope_ref, slopel_ref, u_ref, q_ref, qt_ref, k_ref, kt_ref, v_ref, vt_ref,
    p_ref, d_ref, pl_ref, dl_ref, att_ref, do_ref, dot_ref, dk_ref, dv_ref, dkl_ref, dvl_ref,
    pg_ref, pgl_ref,
):
    seq = seq_ref[0]
    col = col_ref[0]
    length = lengths_ref[col]
    base = seq * HALF
    upper = seq == 1
    active = length > base
    lanes = lax.broadcasted_iota(jnp.int32, (1, 2 * DH), 1)
    head_mask = [(lanes < DH).astype(f32).astype(bf16), (lanes >= DH).astype(f32).astype(bf16)]
    loads = [
        pltpu.make_async_copy(src, dst, sems.at[n])
        for n, (src, dst) in enumerate(((w_hbm, w_ref), (wo_hbm, wo_ref), (cot_hbm, cot_ref)))
    ]
    for load in loads:
        load.start()
    QB = HALF // 2
    parts = [slice(0, QB), slice(QB, HALF)]

    def place(half, b):
        i = 2 * half + b // 2
        return (b + col) & 1, pl.multiple_of(i * BLK, BLK)

    def features(half):
        parts = []
        for b in range(NBLK):
            src, at = place(half, b)
            part = e_ref[:, src, :, pl.ds(at, BLK)].astype(f32).reshape(D, BLK)
            parts.append(part.T)
        return jnp.concatenate(parts, axis=0)

    def put_grad(half, grad):
        flat = grad.T.reshape(D // FEAT, FEAT, HALF).astype(bf16)
        for b in range(NBLK):
            dst, at = place(half, b)
            g_ref[:, dst, :, pl.ds(at, BLK)] = flat[:, :, b * BLK : (b + 1) * BLK]

    def pairs_of(act):
        return [act[:, hp * 2 * DH : (hp + 1) * 2 * DH] for hp in range(PAIRS)]

    def project(half, blocks, yb, slopes):
        for n, blk in enumerate(blocks):
            act, slope = gate(dot_nn(yb, w_ref[:, blk * HID : (blk + 1) * HID]))
            slopes[:, n * HID : (n + 1) * HID] = slope
            act = act.astype(bf16)
            if blk == 0:
                u_ref[...] = act
            elif blk == 2:
                act = act.astype(f32) * (0.5 * DH**-0.5)
                qt_ref[...] = act.T.astype(bf16)
                for hp, part in enumerate(pairs_of(act.astype(bf16))):
                    q_ref[hp] = part
            else:
                target, turned = (v_ref, vt_ref) if blk == 1 else (k_ref, kt_ref)
                turned[half] = act.T
                for hp, part in enumerate(pairs_of(act)):
                    target[half, hp] = part

    def plus(a, b):
        return b if a is None else a + b

    def blocks_of(lower):
        keys = {0: (0,), 1: (0, 1)}
        low = (-1,) if lower else ()
        return [(h, qi, ki) for h in range(2) for qi in range(2) for ki in keys[qi] + low]

    def ahead(first, second, tasks):
        ready = [first(*task) for task in tasks[:AHEAD]]
        for n, task in enumerate(tasks):
            if n + AHEAD < len(tasks):
                ready.append(first(*tasks[n + AHEAD]))
            second(*task, ready[n])

    def rows_of(hp, h):
        head = 2 * hp + h
        return head, pl.ds(pl.multiple_of(head * DH, DH), DH)

    def forward(hp, lower):
        q, k = q_ref[hp], k_ref[1, hp]
        qm = [q * head_mask[h] for h in range(2)]
        row = lax.broadcasted_iota(jnp.int32, (QB, 1), 0)
        att = {}

        def first(h, qi, ki):
            return dot_nt(qm[h][parts[qi]], k_ref[0, hp] if ki < 0 else k[parts[ki]])

        def second(h, qi, ki, half):
            head, hs = rows_of(hp, h)
            a = 1.0 + jnp.tanh(half)
            if ki == qi:
                limit = jnp.minimum(row, length - 1 - base - ki * QB)
                ok = lax.broadcasted_iota(jnp.int32, a.shape, 1) <= limit
                a = jnp.where(ok, a, 0.0)
            p = (half * a).astype(bf16)
            if ki < 0:
                pl_ref[head, parts[qi]] = p
                dl_ref[head, parts[qi]] = a
                vt = vt_ref[0, hs, :]
            else:
                p_ref[head, 2 * qi + ki] = p
                d_ref[head, 2 * qi + ki] = a
                vt = vt_ref[1, hs, parts[ki]]
            att[h, qi] = plus(att.get((h, qi)), dot_nt(vt, p))

        ahead(first, second, blocks_of(lower))
        for h in range(2):
            att_ref[rows_of(hp, h)[1], :] = jnp.concatenate([att[h, 0], att[h, 1]], axis=1)

    def backward(hp, lower):
        v, do = v_ref[1, hp], do_ref[hp]
        dm = [do * head_mask[h] for h in range(2)]
        dq, dk, dv = {}, {}, {}

        def first(h, qi, ki):
            return dot_nt(dm[h][parts[qi]], v_ref[0, hp] if ki < 0 else v[parts[ki]])

        def second(h, qi, ki, dp):
            head, hs = rows_of(hp, h)
            qs = parts[qi]
            if ki < 0:
                p, a = pl_ref[head, qs], dl_ref[head, qs]
                kt = kt_ref[0, hs, :]
            else:
                p, a = p_ref[head, 2 * qi + ki], d_ref[head, 2 * qi + ki]
                kt = kt_ref[1, hs, parts[ki]]
            ds = (dp * slope_of(a, p)).astype(bf16)
            dq[h, qi] = plus(dq.get((h, qi)), dot_nt(kt, ds))
            dk[h, ki] = plus(dk.get((h, ki)), dot_nn(qt_ref[hs, qs], ds))
            dv[h, ki] = plus(dv.get((h, ki)), dot_nn(dot_ref[hs, qs], p))

        ahead(first, second, blocks_of(lower))
        for h in range(2):
            hs = rows_of(hp, h)[1]
            att_ref[hs, :] = jnp.concatenate([dq[h, 0], dq[h, 1]], axis=1)
            dk_ref[hs, :] = jnp.concatenate([dk[h, 0], dk[h, 1]], axis=1)
            dv_ref[hs, :] = jnp.concatenate([dv[h, 0], dv[h, 1]], axis=1)
            if lower:
                dkl_ref[hs, :] = dk[h, -1]
                dvl_ref[hs, :] = dv[h, -1]

    def over_pairs(body):
        @pl.when(upper)
        def _():
            @pl.loop(0, PAIRS)
            def _(hp):
                body(hp, True)

        @pl.when(jnp.logical_not(upper))
        def _():
            @pl.loop(0, PAIRS)
            def _(hp):
                body(hp, False)

    g_ref[...] = jnp.zeros_like(g_ref)

    @pl.when(jnp.logical_not(active))
    def _():
        for load in loads:
            load.wait()
        out_ref[...] = jnp.zeros_like(out_ref)

    @pl.when(active)
    def _():
        x = features(seq)
        for load in loads:
            load.wait()
        x_ref[...] = x
        y, r = norm(x)
        y_ref[...] = y
        r_ref[...] = 0.5 * r
        project(1, (0, 1, 2, 3), (0.5 * y).astype(bf16), slope_ref)

        @pl.when(upper)
        def _():
            y, r = norm(features(0))
            yl_ref[...] = y
            rl_ref[...] = 0.5 * r
            project(0, (1, 3), (0.5 * y).astype(bf16), slopel_ref)

        over_pairs(forward)

        na, ra = norm(att_ref[...].T * (1.0 / LEN))
        u = u_ref[...].astype(f32)
        valid = (base + lax.broadcasted_iota(jnp.int32, (HALF, 1), 0)) < length
        mixed = dot_nn((na * u).astype(bf16), wo_ref[...]) + x_ref[...]
        out_ref[...] = jnp.where(valid, mixed, 0.0).astype(bf16)
        cot = jnp.where(valid, cot_ref[...].astype(f32), 0.0)
        gg = dot_nt(cot.astype(bf16), wo_ref[...])
        pg_ref[:, :HID] = (gg * na * slope_ref[:, :HID]).astype(bf16)
        da = norm_back(na, ra * (1.0 / LEN), gg * u)
        dot_ref[...] = da.T.astype(bf16)
        for hp, part in enumerate(pairs_of(da.astype(bf16))):
            do_ref[hp] = part

        over_pairs(backward)

        dq = att_ref[...].T * (0.5 * DH**-0.5)
        pg_ref[:, HID : 2 * HID] = (dv_ref[...].T * slope_ref[:, HID : 2 * HID]).astype(bf16)
        pg_ref[:, 2 * HID : 3 * HID] = (dq * slope_ref[:, 2 * HID : 3 * HID]).astype(bf16)
        pg_ref[:, 3 * HID :] = (dk_ref[...].T * slope_ref[:, 3 * HID :]).astype(bf16)
        eg = dot_nt(pg_ref[...], w_ref[...])
        cot = jnp.where(valid, cot_ref[...].astype(f32), 0.0)
        put_grad(seq, cot + norm_back(y_ref[...], r_ref[...], eg))

        @pl.when(upper)
        def _():
            pgl_ref[:, :HID] = (dvl_ref[...].T * slopel_ref[:, :HID]).astype(bf16)
            pgl_ref[:, HID:] = (dkl_ref[...].T * slopel_ref[:, HID:]).astype(bf16)
            eg = dot_nt(pgl_ref[:, :HID], w_ref[:, HID : 2 * HID])
            eg = eg + dot_nt(pgl_ref[:, HID:], w_ref[:, 3 * HID :])
            put_grad(0, norm_back(yl_ref[...], rl_ref[...], eg))


def vmem():
    return pl.BlockSpec(memory_space=pltpu.VMEM)


def hbm():
    return pl.BlockSpec(memory_space=pl.ANY)


def smem():
    return pl.BlockSpec(memory_space=pltpu.SMEM)


def in_vmem(x):
    return pltpu.with_memory_space_constraint(x, pltpu.VMEM)


def params():
    return pltpu.CompilerParams(vmem_limit_bytes=60 * 1024 * 1024)


def table_rows(table):
    return pl.pallas_call(
        rows_kernel,
        in_specs=[vmem()],
        out_specs=vmem(),
        out_shape=pltpu.VMEM((G_HI, BLK), f32),
        compiler_params=params(),
        name="table_rows",
    )(table)


def gather(seq, lengths, own, other, rows):
    return pl.pallas_call(
        gather_kernel,
        in_specs=[smem(), smem(), vmem(), vmem(), vmem()],
        out_specs=vmem(),
        out_shape=pltpu.VMEM((USERS, 2, FEAT, HALF), bf16),
        scratch_shapes=[
            pltpu.VMEM((2, NBLK, USERS, BLK), jnp.int32),
            pltpu.VMEM((2, G_STEP, BLK), jnp.int32),
            pltpu.VMEM((2, G_STEP * BLK, BLK), f32),
            pltpu.SMEM((USERS * NBLK + NBLK,), jnp.int32),
            pltpu.SMEM((2, G_STEP, BLK), jnp.int32),
            pltpu.SemaphoreType.DMA((2,)),
        ],
        compiler_params=params(),
        name="gather",
    )(seq, lengths, own, other, rows)


def scatter(seq, lengths, half, own, other, grad, dtype):
    return pl.pallas_call(
        scatter_kernel,
        in_specs=[smem(), smem(), smem(), vmem(), vmem(), vmem()],
        out_specs=vmem(),
        out_shape=pltpu.VMEM((FEAT, S_ROWS), dtype),
        scratch_shapes=[
            pltpu.VMEM((2, NBLK, USERS, BLK), jnp.int32),
            pltpu.VMEM((S_LO * FEAT, S_HI), f32),
            pltpu.SMEM((USERS * NBLK + NBLK,), jnp.int32),
        ],
        compiler_params=params(),
        name="scatter",
    )(seq, lengths, half, own, other, grad)


def layer(seq, col, lengths, e, w, wo, cot):
    return pl.pallas_call(
        layer_kernel,
        in_specs=[smem(), smem(), smem(), vmem(), hbm(), hbm(), hbm()],
        out_specs=(vmem(), vmem()),
        out_shape=(
            jax.ShapeDtypeStruct((HALF, D), bf16),
            pltpu.VMEM((USERS, 2, FEAT, HALF), bf16),
        ),
        scratch_shapes=[
            pltpu.VMEM((D, 4 * HID), bf16),
            pltpu.VMEM((HID, D), bf16),
            pltpu.VMEM((HALF, D), bf16),
            pltpu.SemaphoreType.DMA((3,)),
            pltpu.VMEM((HALF, D), f32),
            pltpu.VMEM((HALF, D), f32),
            pltpu.VMEM((HALF, 1), f32),
            pltpu.VMEM((HALF, D), f32),
            pltpu.VMEM((HALF, 1), f32),
            pltpu.VMEM((HALF, 4 * HID), f32),
            pltpu.VMEM((HALF, 2 * HID), f32),
            pltpu.VMEM((HALF, HID), bf16),
            pltpu.VMEM((PAIRS, HALF, 2 * DH), bf16),
            pltpu.VMEM((HID, HALF), bf16),
            pltpu.VMEM((2, PAIRS, HALF, 2 * DH), bf16),
            pltpu.VMEM((2, HID, HALF), bf16),
            pltpu.VMEM((2, PAIRS, HALF, 2 * DH), bf16),
            pltpu.VMEM((2, HID, HALF), bf16),
            pltpu.VMEM((H, 4, HALF // 2, HALF // 2), bf16),
            pltpu.VMEM((H, 4, HALF // 2, HALF // 2), f32),
            pltpu.VMEM((H, HALF, HALF), bf16),
            pltpu.VMEM((H, HALF, HALF), f32),
            pltpu.VMEM((HID, HALF), f32),
            pltpu.VMEM((PAIRS, HALF, 2 * DH), bf16),
            pltpu.VMEM((HID, HALF), bf16),
            pltpu.VMEM((HID, HALF), f32),
            pltpu.VMEM((HID, HALF), f32),
            pltpu.VMEM((HID, HALF), f32),
            pltpu.VMEM((HID, HALF), f32),
            pltpu.VMEM((HALF, 4 * HID), bf16),
            pltpu.VMEM((HALF, 2 * HID), bf16),
        ],
        compiler_params=params(),
        name="layer",
    )(seq, col, lengths, e, w, wo, cot)


def per_device(history_items, lengths, item_table, input_weight, output_weight, output_cotangent):
    col = lax.axis_index("col").astype(jnp.int32).reshape(1)
    seq = lax.axis_index("seq").astype(jnp.int32).reshape(1)
    swap = [(0, 1), (1, 0)]
    both = ("col", "seq")
    own = history_items
    other = in_vmem(lax.ppermute(own, "seq", swap))
    rows = in_vmem(table_rows(item_table))
    looked = gather(seq, lengths, own, other, rows)
    flat = looked.reshape(2 * USERS, FEAT, HALF)
    arrived = lax.all_to_all(flat, both, split_axis=0, concat_axis=0, tiled=True)
    arrived = in_vmem(arrived.reshape(USERS, 2, FEAT, HALF))
    out, grad = layer(
        seq, col, lengths, arrived, input_weight, output_weight, output_cotangent[0]
    )
    grad = grad.reshape(2 * USERS, FEAT, HALF)
    back = lax.all_to_all(grad, both, split_axis=0, concat_axis=0, tiled=True)
    back = in_vmem(back.reshape(USERS, 2, FEAT, HALF))
    theirs = scatter(seq, lengths, 1 - seq, own, other, back, bf16)
    received = lax.ppermute(theirs, "seq", swap)
    mine = scatter(seq, lengths, seq, own, other, back, f32)
    return (out[None], mine + received.astype(f32))


def solution(mesh):
    in_specs = (P(None, "seq"), P(), P("col", None), P(), P(), P("col", "seq", None))
    out_specs = (P("col", "seq", None), P("col", "seq"))
    return jax.shard_map(
        per_device, mesh=mesh, in_specs=in_specs, out_specs=out_specs, check_vma=False
    )
```
